32 devices in a mesh: seq: 16 (over z, x, core), tp: 2 (over y).
Axes of the slice: x: 2, y: 2, z: 4, core: 2. Of those that a mesh axis runs over, the one named last changes fastest.
Arguments:
- tokens: bfloat16 [2048, 2048], P('seq', 'tp'), may hold values from -6 to 6
- attn_gain: bfloat16 [2048], replicated, may hold values from 0.25 to 1.75
- w_query: bfloat16 [2048, 2048], P(None, 'tp'), may hold values from -1 to 9
- w_key: bfloat16 [2048, 2048], P(None, 'tp'), may hold values from -0.125 to 0.125
- w_value: bfloat16 [2048, 2048], P(None, 'tp'), may hold values from -0.125 to 0.125
- w_out: bfloat16 [2048, 2048], P('tp'), may hold values from -0.5 to 0.5
- prefix_keys: bfloat16 [512, 2048], P('seq', 'tp'), may hold values from -6 to 6
- prefix_values: bfloat16 [512, 2048], P('seq', 'tp'), may hold values from -6 to 6
- shard_group: int32 [16], replicated, may hold values from 0 to 1, as said below
- request_group: int32 [8], replicated, may hold values from 0 to 1, as said below
- lengths: int32 [8], replicated, may hold values from 1 to 512, 2048 in all
- moe_gain: bfloat16 [2048], replicated, may hold values from 0.25 to 1.75
- w_router: bfloat16 [2048, 16], replicated, may hold values from -1 to 8
- w_gate: bfloat16 [16, 2048, 1024], P('seq', None, 'tp'), may hold values from -0.125 to 0.125
- w_up: bfloat16 [16, 2048, 1024], P('seq', None, 'tp'), may hold values from -0.125 to 0.125
- w_down: bfloat16 [16, 1024, 2048], P('seq', 'tp'), may hold values from -3 to 3
- routes: int32 [2048, 8], P('seq'), may hold values from 0 to 15, all different within a row; in each aligned block of 128 rows (0 to 127, 128 to 255, ...) at most 96 rows name the same one
- final_gain: bfloat16 [2048], P('tp'), may hold values from 0.25 to 1.75
- w_head: bfloat16 [2048, 50304], P('tp', 'seq'), may hold values from -2 to 9
Outputs:
- hidden: bfloat16 [2048, 2048], P('seq', 'tp')
- log_probs: float32 [8, 50304], P(None, 'seq')
The draws below stay inside these ranges and needn't reach their ends.
Inputs may be any that keep to these rules, and one draw needn't show every extreme that they name: `shard_group`: exactly half of the 16 cache shards belong to each group. `request_group`: exactly half of the requests belong to each group. The lengths sum to 2048; the largest is exactly 512. `routes`: among the rows of one device no expert is named more than 96 times, a bound that some block reaches.
All inputs are finite; a program needn't handle non-finite values.
Results may differ from the reference program's by a relative error of at most 0.017.
The reference program's roundings to bfloat16 on the way count: a program that leaves them out, or rounds other values in their place, can miss the bound.
Values may be sent and summed in bfloat16 or wider, within the bound.
A program may use at most 128 MiB of HBM per device.

```python
import math
import jax
import jax.numpy as jnp
import numpy as np
from jax import lax

D = 2048
HEADS = 16
HD = 128
FFE = 1024
VOCAB = 50304
TOPK = 8
SPAN = 4
TOK_DEV = 128
PDEV = 32
EXPERTS = 16
TOKENS = 2048
REQS = 8
PREFIX = 256
CAP = 96
N_SEQ = 16


def draw_shard_group(key, part):
    order = jax.random.permutation(jax.random.fold_in(key, 11), N_SEQ)
    return (order < N_SEQ // 2).astype(jnp.int32)


def draw_request_group(key, part):
    order = jax.random.permutation(jax.random.fold_in(key, 23), REQS)
    return (order % 2).astype(jnp.int32)


def draw_tokens(key, part):
    noise_key = jax.random.fold_in(key, 31)
    column_frac = jnp.arange(D).astype(jnp.float32)[None, :] / D
    rising = 0.6 + 1.2 * column_frac
    values = jax.random.truncated_normal(noise_key, -3.3, 3.3, (TOKENS, D), jnp.float32) * rising
    return values.astype(jnp.bfloat16)


def draw_w_query(key, part):
    base_key = jax.random.fold_in(key, 43)
    extent = (D, HEADS * HD)
    values = jax.random.truncated_normal(base_key, -4.0, 4.0, extent, jnp.float32) * D ** (-0.5)
    return values.astype(jnp.bfloat16)


def draw_prefix_keys(key, part):
    base_key = jax.random.fold_in(key, 53)
    extent = (N_SEQ * PDEV, HEADS * HD)
    values = jax.random.truncated_normal(base_key, -6.0, 6.0, extent, jnp.float32)
    return values.astype(jnp.bfloat16)


def draw_w_router(key, part):
    base_key = jax.random.fold_in(key, 61)
    extent = (D, EXPERTS)
    values = jax.random.truncated_normal(base_key, -4.0, 4.0, extent, jnp.float32) * D ** (-0.5)
    return values.astype(jnp.bfloat16)


def draw_w_head(key, part):
    base_key = jax.random.fold_in(key, 73)
    extent = (D, VOCAB)
    column_pos = jnp.arange(VOCAB)
    rising = 1.0 + 2.0 * column_pos.astype(jnp.float32) / VOCAB
    values = jax.random.truncated_normal(base_key, -6.0, 6.0, extent, jnp.float32) * 0.07 * rising[None, :]
    return values.astype(jnp.bfloat16)


def steps_of(own_key, shape, cuts, smallest, top_value):
    level = 1.0
    for dim, blocks in cuts:
        heights = jax.random.uniform(jax.random.fold_in(jax.random.fold_in(own_key, 6), dim), (blocks,), jnp.float32, smallest / len(cuts), top_value / len(cuts))
        level = level * jnp.repeat(jnp.exp(heights), shape[dim] // blocks).reshape((-1,) + (1,) * (len(shape) - 1 - dim))
    return level


def length_profile(count, total, limit, lean):
    loads = [(1 << 20) // math.isqrt(standing ** lean) + 1 for standing in range(2, count + 1)]
    spare, given = total - limit - (count - 1), [1] * (count - 1)
    while spare > 0:
        candidates = [i for i in range(count - 1) if given[i] < limit]
        whole, remaining = sum([loads[i] for i in candidates]), spare
        for i in candidates:
            extra = min(limit - given[i], max(1, remaining * loads[i] // whole), spare)
            given[i] = given[i] + extra
            spare = spare - extra
    return np.array([limit] + given)


def ragged_sizes(stream_key, count, total, bound, skew):
    if count == 2:
        one = jax.random.randint(stream_key, (), max(1, total - bound), min(bound, total - 1) + 1)
        return jnp.stack([one, total - one])
    sizes = jnp.asarray(length_profile(count, total, bound, skew), jnp.int32)
    pairs = (count - 1) // 2
    source_of, taker = sizes[1:1 + 2 * pairs:2], sizes[2:2 + 2 * pairs:2]
    slack = jnp.minimum(source_of - 1, bound - taker)
    passed = jax.random.randint(jax.random.fold_in(stream_key, 1), (pairs,), 0, 1 << 20) % (slack + 1)
    sizes = sizes.at[1:1 + 2 * pairs:2].set(source_of - passed).at[2:2 + 2 * pairs:2].set(taker + passed)
    return sizes[jax.random.permutation(jax.random.fold_in(stream_key, 2), count)]


def routed_block(stream_key, own, number, rows, number_of, top, bound, slope):
    sequence = jax.random.permutation(stream_key, number_of)
    crowded, usual = shares(number_of, rows * top, bound, slope, True), shares(number_of, rows * top, bound, slope, False)
    places = jnp.arange(number_of)

    def named(sizes, turn):
        used = int((sizes > 0).sum())
        fixed = max(1, used // 4)
        shifted = fixed + (places - fixed + turn * (used - fixed)) % max(1, number_of - fixed)
        return jnp.zeros((number_of,), jnp.int32).at[sequence[jnp.where(places < fixed, places, shifted)]].set(jnp.asarray(sizes, jnp.int32))

    sizes = jnp.where(number % 4 == 0, named(crowded, number // 4), named(usual, number - number // 4 - 1))
    mixed = jax.random.permutation(jax.random.fold_in(own, 3), number_of)
    donor, sink = mixed[0:number_of // 2 * 2:2], mixed[1:number_of // 2 * 2:2]
    slack = jnp.minimum(sizes[donor] - 1, bound - sizes[sink]) // 2
    slack = jnp.where((donor == sequence[0]) | (sink == sequence[0]) | (sizes[sink] == 0), 0, jnp.maximum(slack, 0))
    shifted = jax.random.randint(jax.random.fold_in(own, 4), (number_of // 2,), 0, 1 << 20) % (slack + 1)
    sizes = sizes.at[donor].add(-shifted).at[sink].add(shifted)
    items = jnp.searchsorted(jnp.cumsum(sizes), jnp.arange(rows * top), side="right").astype(jnp.int32)
    listing = items.reshape(top, rows).T
    listing = listing[jax.random.permutation(jax.random.fold_in(own, 1), rows)]
    turn = jax.random.randint(jax.random.fold_in(own, 2), (rows, 1), 0, top)
    return jnp.take_along_axis(listing, (jnp.arange(top)[None, :] + turn) % top, axis=1)


def shares(number_of, total, most, slope, full):
    portions = [(1 << 20) // math.isqrt(rank ** slope) + 1 for rank in range(1, number_of + 1)]
    largest = most if full else min(most, max(-(-total // number_of), total * portions[0] // sum(portions)))
    least = 1 if total - largest >= number_of - 1 else 0
    holding, surplus = [largest] + [least] * (number_of - 1), total - largest - least * (number_of - 1)
    while surplus > 0:
        candidates = [i for i in range(1, number_of) if holding[i] < largest] or [i for i in range(1, number_of) if holding[i] < most]
        whole, remaining = sum([portions[i] for i in candidates]), surplus
        for i in candidates:
            extra = min(most - holding[i], max(1, remaining * portions[i] // whole), surplus)
            holding[i] = holding[i] + extra
            surplus = surplus - extra
    return np.array(holding)


def scatter_about(stream_key, shape, deviation, reach, cuts=(), dtype=jnp.bfloat16):
    level = steps_of(stream_key, shape, cuts, -0.22, 0.18) if cuts else 1.0
    result = jax.random.normal(stream_key, shape, jnp.float32) * deviation * level
    return jnp.minimum(jnp.maximum(result, -reach), reach).astype(dtype)


def setup_inputs(seed: int = 0) -> dict:
    streams_of = jax.random.split(jax.random.key(seed), 20)
    tokens = draw_tokens(jax.random.fold_in(streams_of[19], 71), 0)
    attn_gain = jnp.clip(1.0 + 0.15 * jax.random.normal(streams_of[1], (D,), jnp.float32), 0.25, 1.75).astype(jnp.bfloat16)
    w_query = draw_w_query(jax.random.fold_in(streams_of[19], 71), 0)
    w_key = scatter_about(streams_of[3], (D, HEADS * HD), D ** -0.5, 0.125, ((1, 2),))
    w_value = scatter_about(streams_of[4], (D, HEADS * HD), D ** -0.5, 0.125, ((1, 2),))
    w_out = scatter_about(streams_of[5], (HEADS * HD, D), (max(1, HEADS * HD // 16)) ** -0.5, 0.5, ((0, 2),))
    prefix_keys = draw_prefix_keys(jax.random.fold_in(streams_of[19], 71), 0)
    prefix_values = scatter_about(streams_of[7], (N_SEQ * PDEV, HEADS * HD), 1.0, 6.0, ((0, 16), (1, 2)))
    shard_group = draw_shard_group(jax.random.fold_in(streams_of[19], 71), 0)
    request_group = draw_request_group(jax.random.fold_in(streams_of[19], 71), 0)
    lengths = ragged_sizes(streams_of[10], REQS, TOKENS, SPAN * TOK_DEV, 2).astype(jnp.int32)
    moe_gain = jnp.clip(1.0 + 0.15 * jax.random.normal(streams_of[11], (D,), jnp.float32), 0.25, 1.75).astype(jnp.bfloat16)
    w_router = draw_w_router(jax.random.fold_in(streams_of[19], 71), 0)
    w_gate = scatter_about(streams_of[13], (EXPERTS, D, FFE), D ** -0.5, 0.125, ((0, 16), (2, 2)))
    w_up = scatter_about(streams_of[14], (EXPERTS, D, FFE), D ** -0.5, 0.125, ((0, 16), (2, 2)))
    w_down = scatter_about(streams_of[15], (EXPERTS, FFE, D), (max(1, FFE // 256)) ** -0.5, 3.0, ((0, 16), (1, 2)))
    routes_keys = jax.random.split(jax.random.fold_in(streams_of[16], 1), TOKENS // TOK_DEV)
    routes_turns = jax.random.permutation(jax.random.fold_in(streams_of[16], 3), TOKENS // TOK_DEV)
    routes = jax.vmap(lambda own, number: routed_block(jax.random.fold_in(streams_of[16], 2), own, number, TOK_DEV, EXPERTS, TOPK, CAP, 2))(routes_keys, routes_turns).reshape((TOKENS, TOPK))
    final_gain = jnp.clip(1.0 + 0.15 * jax.random.normal(streams_of[17], (D,), jnp.float32), 0.25, 1.75).astype(jnp.bfloat16)
    w_head = draw_w_head(jax.random.fold_in(streams_of[19], 71), 0)
    return {"tokens": tokens, "attn_gain": attn_gain, "w_query": w_query, "w_key": w_key, "w_value": w_value, "w_out": w_out, "prefix_keys": prefix_keys, "prefix_values": prefix_values, "shard_group": shard_group, "request_group": request_group, "lengths": lengths, "moe_gain": moe_gain, "w_router": w_router, "w_gate": w_gate, "w_up": w_up, "w_down": w_down, "routes": routes, "final_gain": final_gain, "w_head": w_head}


EPS = 1e-05

def normalize(rows, gain):
    inv = lax.rsqrt(lax.optimization_barrier(jnp.mean(rows * rows, -1, keepdims=True)) + EPS)
    return rows * inv * gain.astype(jnp.float32)

def rotate(vectors, position):
    half = vectors.shape[-1] // 2
    freq = 10000.0 ** (-jnp.arange(half).astype(jnp.float32) / half)
    angle = position[:, None] * freq[None, :]
    cosine = jnp.cos(angle)[:, None, :]
    sine = jnp.sin(angle)[:, None, :]
    first = vectors[..., :half]
    second = vectors[..., half:]
    return jnp.concatenate([first * cosine - second * sine, second * cosine + first * sine], -1)

def reference(tokens, attn_gain, w_query, w_key, w_value, w_out, prefix_keys, prefix_values, shard_group, request_group, lengths, moe_gain, w_router, w_gate, w_up, w_down, routes, final_gain, w_head):
    f32 = jnp.float32
    bf16 = jnp.bfloat16
    ends = jnp.cumsum(lengths).astype(jnp.int32)
    starts = ends - lengths
    index = jnp.arange(TOKENS).astype(jnp.int32)
    request = lax.optimization_barrier(jnp.sum((index[:, None] >= ends[None, :]).astype(jnp.int32), 1))
    position = (PREFIX + index - starts[request]).astype(f32)
    group = request_group[request]
    cache_group = shard_group[jnp.arange(N_SEQ * PDEV).astype(jnp.int32) // PDEV]
    normed = normalize(tokens.astype(f32), attn_gain).astype(bf16)
    query = rotate(jnp.dot(normed, w_query, preferred_element_type=f32).reshape(TOKENS, HEADS, HD), position).astype(bf16)
    key = rotate(jnp.dot(normed, w_key, preferred_element_type=f32).reshape(TOKENS, HEADS, HD), position).astype(bf16)
    value = jnp.dot(normed, w_value, preferred_element_type=f32).astype(bf16).reshape(TOKENS, HEADS, HD)
    cache_k = prefix_keys.reshape(N_SEQ * PDEV, HEADS, HD)
    cache_v = prefix_values.reshape(N_SEQ * PDEV, HEADS, HD)
    prefix_mask = group[:, None] == cache_group[None, :]
    suffix_mask = (request[:, None] == request[None, :]) & (index[None, :] <= index[:, None])
    allowed = jnp.concatenate([prefix_mask, suffix_mask], 1)

    def one_head(head):
        qh = query[:, head, :].astype(f32)
        kh = jnp.concatenate([cache_k[:, head, :], key[:, head, :]], 0).astype(f32)
        vh = jnp.concatenate([cache_v[:, head, :], value[:, head, :]], 0)
        scores = jnp.dot(qh, kh.T) / jnp.sqrt(f32(HD))
        scores = jnp.where(allowed, scores, -jnp.inf)
        peak = lax.optimization_barrier(jnp.max(scores, -1, keepdims=True))
        weights = jnp.where(allowed, jnp.exp(scores - peak), 0.0)
        total = lax.optimization_barrier(jnp.sum(weights, -1, keepdims=True))
        summed = jnp.dot(weights.astype(bf16).astype(f32), vh.astype(f32))
        return (summed / total).astype(bf16)
    attended = lax.map(one_head, jnp.arange(HEADS))
    attended = jnp.transpose(attended, (1, 0, 2)).reshape(TOKENS, HEADS * HD)
    resid = (tokens.astype(f32) + jnp.dot(attended, w_out, preferred_element_type=f32)).astype(bf16)
    moe_in = normalize(resid.astype(f32), moe_gain).astype(bf16)
    probs = jax.nn.softmax(jnp.dot(moe_in, w_router, preferred_element_type=f32), -1)
    route_weight = jnp.take_along_axis(probs, routes, 1)
    flat = routes.reshape(N_SEQ, TOK_DEV * TOPK)
    hits = (flat[:, :, None] == jnp.arange(EXPERTS).astype(jnp.int32)[None, None, :]).astype(jnp.int32)
    rank = lax.optimization_barrier(jnp.sum((jnp.cumsum(hits, 1) - hits) * hits, -1))
    block = jnp.broadcast_to(jnp.arange(N_SEQ).astype(jnp.int32)[:, None], flat.shape)
    token_id = block * TOK_DEV + jnp.arange(TOK_DEV * TOPK).astype(jnp.int32)[None, :] // TOPK
    table = jnp.zeros((EXPERTS, N_SEQ, CAP), jnp.int32).at[flat, block, rank].set(token_id)

    def one_expert(pack):
        rows_id, gate_w, up_w, down_w = pack
        rows = moe_in[rows_id.reshape(-1)]
        gate = jnp.dot(rows, gate_w, preferred_element_type=f32)
        up = jnp.dot(rows, up_w, preferred_element_type=f32)
        act = (jax.nn.silu(gate) * up).astype(bf16)
        return jnp.dot(act, down_w, preferred_element_type=f32).astype(bf16)
    outputs = lax.map(one_expert, (table, w_gate, w_up, w_down))
    outputs = outputs.reshape(EXPERTS * N_SEQ * CAP, D)
    picked = outputs[((flat * N_SEQ + block) * CAP + rank).reshape(-1)].reshape(TOKENS, TOPK, D)
    moe = lax.optimization_barrier(jnp.sum(picked.astype(f32) * route_weight[:, :, None], 1))
    hidden = (resid.astype(f32) + moe).astype(bf16)
    final = normalize(hidden.astype(f32), final_gain).astype(bf16)
    last = final[ends - 1]
    logits = jnp.dot(last, w_head, preferred_element_type=f32)
    peak = lax.optimization_barrier(jnp.max(logits, -1, keepdims=True))
    log_probs = logits - peak - jnp.log(lax.optimization_barrier(jnp.sum(jnp.exp(logits - peak), -1, keepdims=True)))
    return (hidden, log_probs)
```

```python
import jax
import jax.numpy as jnp
from jax import lax
from jax.sharding import PartitionSpec as P

HD = 128
SPAN = 4


EPS = 1e-05
NEGATIVE = -1e30


def from_behind(value, axis, steps):
    count = lax.axis_size(axis)
    leading, last = (max(0, -steps), min(count, count - steps))
    return lax.ppermute(value, axis, [(source, source + steps) for source in range(leading, last)])


def normalize(rows, gain):
    inv = lax.rsqrt(jnp.mean(rows * rows, -1, keepdims=True) + EPS)
    return rows * inv * gain.astype(jnp.float32)


def rotate(vectors, position):
    half = vectors.shape[-1] // 2
    freq = 10000.0 ** (-jnp.arange(half).astype(jnp.float32) / half)
    angle = position[:, None] * freq[None, :]
    cosine = jnp.cos(angle)[:, None, :]
    sine = jnp.sin(angle)[:, None, :]
    first = vectors[..., :half]
    second = vectors[..., half:]
    return jnp.concatenate([first * cosine - second * sine, second * cosine + first * sine], -1)


def request_of(index, ends):
    return jnp.sum((index[:, None] >= ends[None, :]).astype(jnp.int32), 1)


def lookup(selector, table):
    hit = selector[:, None] == jnp.arange(table.shape[0])[None, :]
    return jnp.sum(jnp.where(hit, table[None, :], 0), 1)


def attend(carry, query, keys, values, allowed):
    best, total, accum = carry
    heads = query.shape[1]
    keys = keys.reshape(keys.shape[0], heads, -1)
    values = values.reshape(values.shape[0], heads, -1)
    scale = query.shape[-1] ** (-0.5)
    scores = jnp.einsum("thd,khd->htk", query, keys, preferred_element_type=jnp.float32) * scale
    scores = jnp.where(allowed[None], scores, NEGATIVE)
    top = jnp.maximum(best, jnp.max(scores, -1))
    factor = jnp.exp(best - top)
    weights = jnp.where(allowed[None], jnp.exp(scores - top[..., None]), 0.0)
    total = factor * total + jnp.sum(weights, -1)
    accum = factor[..., None] * accum + jnp.einsum(
        "htk,khd->htd", weights.astype(jnp.bfloat16), values, preferred_element_type=jnp.float32
    )
    return (top, total, accum)


def on_device(
    tokens,
    attn_gain,
    w_query,
    w_key,
    w_value,
    w_out,
    prefix_keys,
    prefix_values,
    shard_group,
    request_group,
    lengths,
    moe_gain,
    w_router,
    w_gate,
    w_up,
    w_down,
    routes,
    final_gain,
    w_head,
):
    f32 = jnp.float32
    bf16 = jnp.bfloat16
    seq_index = lax.axis_index("seq")
    tp_index = lax.axis_index("tp")
    seq_count = lax.axis_size("seq")
    tp_count = lax.axis_size("tp")
    tok_dev = tokens.shape[0]
    width_part = tokens.shape[1]
    shard_rows = prefix_keys.shape[0]
    prefix_length = shard_rows * seq_count // 2
    full_x = lax.all_gather(tokens, "tp", axis=1, tiled=True)
    width = full_x.shape[1]
    normed = normalize(full_x.astype(f32), attn_gain).astype(bf16)
    heads = w_query.shape[1] // HD
    ends = jnp.cumsum(lengths)
    starts = ends - lengths
    local_index = seq_index * tok_dev + jnp.arange(tok_dev)
    own_request = request_of(local_index, ends)
    own_start = lookup(own_request, starts)
    own_group = lookup(own_request, request_group)
    position = (prefix_length + local_index - own_start).astype(f32)
    query = rotate(
        jnp.dot(normed, w_query, preferred_element_type=f32).reshape(tok_dev, heads, HD), position
    ).astype(bf16)
    key_rows = rotate(
        jnp.dot(normed, w_key, preferred_element_type=f32).reshape(tok_dev, heads, HD), position
    ).astype(bf16)
    key_rows = key_rows.reshape(tok_dev, heads * HD)
    value_rows = jnp.dot(normed, w_value, preferred_element_type=f32).astype(bf16)
    start_state = (
        jnp.full((heads, tok_dev), NEGATIVE, f32),
        jnp.zeros((heads, tok_dev), f32),
        jnp.zeros((heads, tok_dev, HD), f32),
    )
    pieces = (
        lax.all_gather(prefix_keys, "seq", axis=0, tiled=True),
        lax.all_gather(prefix_values, "seq", axis=0, tiled=True),
    )
    count = pieces[0].shape[0]
    shard_ids = jnp.arange(count) // shard_rows
    key_group = lookup(shard_ids, shard_group)
    fold_allowed = own_group[:, None] == key_group[None, :]
    state = attend(start_state, query, pieces[0], pieces[1], fold_allowed)
    own_allowed = (own_request[:, None] == own_request[None, :]) & (
        local_index[None, :] <= local_index[:, None]
    )
    state = attend(state, query, key_rows, value_rows, own_allowed)
    both_rows = jnp.concatenate([key_rows, value_rows], 1)
    behind = [from_behind(both_rows, "seq", step) for step in range(1, SPAN + 1)]
    half = heads * HD
    for step in range(1, SPAN + 1):
        moving = behind[step - 1]
        key_index = (seq_index - step) * tok_dev + jnp.arange(tok_dev)
        key_request = request_of(key_index, ends)
        allowed = (key_index >= 0)[None, :] & (own_request[:, None] == key_request[None, :])
        state = attend(state, query, moving[:, :half], moving[:, half:], allowed)
    best, total, accum = state
    attended = (accum / total[..., None]).astype(bf16)
    attended = jnp.transpose(attended, (1, 0, 2)).reshape(tok_dev, heads * HD)
    mixed = jnp.dot(attended, w_out, preferred_element_type=f32).astype(bf16)
    parts = lax.all_gather(mixed, "tp", axis=0)
    resid_full = (full_x.astype(f32) + jnp.sum(parts.astype(f32), 0)).astype(bf16)
    moe_in = normalize(resid_full.astype(f32), moe_gain).astype(bf16)
    resid = lax.dynamic_slice_in_dim(resid_full, tp_index * width_part, width_part, 1)
    experts = w_router.shape[1]
    topk = routes.shape[1]
    probs = jax.nn.softmax(jnp.dot(moe_in, w_router, preferred_element_type=f32), -1)
    if 2 * topk >= experts:
        named = routes[:, :, None] == jnp.arange(experts)[None, None, :]
        share = jnp.sum(jnp.where(named, probs[:, None, :], 0.0), 1)
        shares = lax.all_gather(share, "seq", axis=0, tiled=True)
        own_share = lax.dynamic_slice_in_dim(shares, seq_index, 1, 1)
        rows = lax.all_gather(moe_in, "seq", axis=0, tiled=True)
        gate = jnp.dot(rows, w_gate[0], preferred_element_type=f32)
        up = jnp.dot(rows, w_up[0], preferred_element_type=f32)
        act = (jax.nn.silu(gate) * up).astype(bf16)
        partial_out = (jnp.dot(act, w_down[0], preferred_element_type=f32) * own_share).astype(bf16)
        summed = lax.psum_scatter(partial_out, "seq", scatter_dimension=0, tiled=True)
        moe_part = lax.psum_scatter(summed, "tp", scatter_dimension=1, tiled=True).astype(f32)
    else:
        flat = routes.reshape(-1)
        hits = (flat[:, None] == jnp.arange(experts)[None, :]).astype(jnp.int32)
        rank = jnp.sum((jnp.cumsum(hits, 0) - hits) * hits, 1)
        capacity = min(tok_dev, tp_count * max(1, 3 * tok_dev * topk // (2 * experts * tp_count)))
        target = flat * capacity + rank
        route_weight = jnp.sum(hits.reshape(tok_dev, topk, experts).astype(f32) * probs[:, None, :], -1)
        repeated = jnp.repeat(moe_in, topk, axis=0)
        outgoing = (
            jnp.zeros((experts * capacity, width), bf16)
            .at[target]
            .set(repeated)
            .reshape(experts, capacity, width)
        )
        arrived = lax.all_to_all(outgoing, "seq", split_axis=0, concat_axis=0, tiled=True)
        sources = arrived.shape[0]
        count = arrived.shape[1]
        rows = arrived.reshape(sources * count, width)
        gate = jnp.dot(rows, w_gate[0], preferred_element_type=f32)
        up = jnp.dot(rows, w_up[0], preferred_element_type=f32)
        act = (jax.nn.silu(gate) * up).astype(bf16)
        partial_out = jnp.dot(act, w_down[0], preferred_element_type=f32).reshape(sources, count, width)
        summed = lax.psum_scatter(partial_out, "tp", scatter_dimension=2, tiled=True).astype(bf16)
        returned = lax.all_to_all(summed, "seq", split_axis=0, concat_axis=0, tiled=True)
        picked = returned.reshape(experts * capacity, width_part)[target].reshape(
            tok_dev, topk, width_part
        )
        moe_part = jnp.sum(picked.astype(f32) * route_weight[:, :, None], 1)
    hidden = (resid.astype(f32) + moe_part).astype(bf16)
    last_hit = ((ends - 1)[:, None] == local_index[None, :]).astype(bf16)
    chosen = jnp.dot(last_hit, hidden, preferred_element_type=f32)
    lane_tp = jnp.arange(tp_count)[None, :, None]
    spread = jnp.where(lane_tp == tp_index, chosen[:, None, :], 0.0).reshape(chosen.shape[0], width)
    last = lax.psum(spread, ("seq", "tp"))
    final_sq = jnp.sum(last * last, -1)
    own_last = lax.dynamic_slice_in_dim(last, tp_index * width_part, width_part, 1)
    final = (own_last * lax.rsqrt(final_sq / width + EPS)[:, None] * final_gain.astype(f32)).astype(
        bf16
    )
    logits = lax.psum(jnp.dot(final, w_head, preferred_element_type=f32), "tp")
    peak_own = jnp.max(logits, -1)
    total_own = jnp.sum(jnp.exp(logits - peak_own[:, None]), -1)
    pairs = lax.all_gather(jnp.stack([peak_own, total_own]), "seq", axis=0)
    peak_logit = jnp.max(pairs[:, 0], 0)
    total_exp = jnp.sum(pairs[:, 1] * jnp.exp(pairs[:, 0] - peak_logit[None, :]), 0)
    log_probs = logits - peak_logit[:, None] - jnp.log(total_exp)[:, None]
    return (hidden, log_probs)


def solution(mesh):
    in_specs = (
        P("seq", "tp"),
        P(),
        P(None, "tp"),
        P(None, "tp"),
        P(None, "tp"),
        P("tp", None),
        P("seq", "tp"),
        P("seq", "tp"),
        P(),
        P(),
        P(),
        P(),
        P(),
        P("seq", None, "tp"),
        P("seq", None, "tp"),
        P("seq", "tp", None),
        P("seq", None),
        P("tp"),
        P("tp", "seq"),
    )
    out_specs = (P("seq", "tp"), P(None, "seq"))
    return jax.shard_map(
        on_device, mesh=mesh, in_specs=in_specs, out_specs=out_specs, check_vma=False
    )
```

```python
import jax
import jax.numpy as jnp
from jax import lax
from jax.experimental import pallas as pl
from jax.experimental.pallas import tpu as pltpu
from jax.sharding import PartitionSpec as P

HD = 128
SPAN = 4
VMEM = pltpu.VMEM


EPS = 1e-05
NEGATIVE = -1e30


def from_behind(value, axis, steps):
    count = lax.axis_size(axis)
    leading, last = (max(0, -steps), min(count, count - steps))
    return lax.ppermute(value, axis, [(source, source + steps) for source in range(leading, last)])


def normalize(rows, gain):
    inv = lax.rsqrt(jnp.mean(rows * rows, -1, keepdims=True) + EPS)
    return rows * inv * gain.astype(jnp.float32)


def rotate(vectors, position):
    half = vectors.shape[-1] // 2
    freq = 10000.0 ** (-jnp.arange(half).astype(jnp.float32) / half)
    angle = position[:, None] * freq[None, :]
    cosine = jnp.cos(angle)[:, None, :]
    sine = jnp.sin(angle)[:, None, :]
    first = vectors[..., :half]
    second = vectors[..., half:]
    return jnp.concatenate([first * cosine - second * sine, second * cosine + first * sine], -1)


def request_of(index, ends):
    return jnp.sum((index[:, None] >= ends[None, :]).astype(jnp.int32), 1)


def lookup(selector, table):
    hit = selector[:, None] == jnp.arange(table.shape[0])[None, :]
    return jnp.sum(jnp.where(hit, table[None, :], 0), 1)


def attend(carry, query, keys, values, allowed):
    best, total, accum = carry
    heads = query.shape[1]
    keys = keys.reshape(keys.shape[0], heads, -1)
    values = values.reshape(values.shape[0], heads, -1)
    scale = query.shape[-1] ** (-0.5)
    scores = jnp.einsum("thd,khd->htk", query, keys, preferred_element_type=jnp.float32) * scale
    scores = jnp.where(allowed[None], scores, NEGATIVE)
    top = jnp.maximum(best, jnp.max(scores, -1))
    factor = jnp.exp(best - top)
    weights = jnp.where(allowed[None], jnp.exp(scores - top[..., None]), 0.0)
    total = factor * total + jnp.sum(weights, -1)
    accum = factor[..., None] * accum + jnp.einsum(
        "htk,khd->htd", weights.astype(jnp.bfloat16), values, preferred_element_type=jnp.float32
    )
    return (top, total, accum)


def partner(axis, bit):
    index = lax.axis_index(axis)
    span = 1 << bit
    other = index + span - 2 * span * ((index // span) % 2)
    return {axis: other}


def greet(stages):
    barrier = pltpu.get_barrier_semaphore()
    for axis, bit in stages:
        pl.semaphore_signal(barrier, inc=1, device_id=partner(axis, bit))
    pl.semaphore_wait(barrier, len(stages))


def swap(source, target, send_sem, recv_sem, stage):
    copy = pltpu.make_async_remote_copy(
        src_ref=source, dst_ref=target, send_sem=send_sem, recv_sem=recv_sem,
        device_id=partner(*stage),
    )
    copy.start()
    return copy


def bits_of(axis):
    return [(axis, bit) for bit in range(lax.axis_size(axis).bit_length() - 1)]


def last_rows(chosen, gain, width):
    seq_stages, tp_stages = bits_of("seq"), bits_of("tp")
    stages = seq_stages + tp_stages
    rows, part = chosen.shape

    def kernel(chosen_ref, gain_ref, out_ref, held, got, sq_held, sq_got, send_sem, recv_sem):
        greet(stages)
        held[0] = chosen_ref[...]
        count = len(seq_stages)
        for k, stage in enumerate(seq_stages):
            swap(held.at[k], got.at[k], send_sem.at[k], recv_sem.at[k], stage).wait()
            held[k + 1] = held[k] + got[k]
        total = held[count]
        sq_held[0] = jnp.broadcast_to(jnp.sum(total * total, -1, keepdims=True), (rows, 128))
        for k, stage in enumerate(tp_stages):
            n = count + k
            swap(sq_held.at[k], sq_got.at[k], send_sem.at[n], recv_sem.at[n], stage).wait()
            sq_held[k + 1] = sq_held[k] + sq_got[k]
        square = sq_held[len(tp_stages)][:, :1]
        scaled = total * lax.rsqrt(square / width + EPS) * gain_ref[...].astype(jnp.float32)
        out_ref[...] = scaled.astype(jnp.bfloat16)

    ns, nt = len(seq_stages), len(tp_stages)
    return pl.pallas_call(
        kernel,
        out_shape=jax.ShapeDtypeStruct((rows, part), jnp.bfloat16),
        in_specs=[pl.BlockSpec(memory_space=VMEM)] * 2,
        out_specs=pl.BlockSpec(memory_space=VMEM),
        scratch_shapes=[
            VMEM((ns + 1, rows, part), jnp.float32),
            VMEM((ns, rows, part), jnp.float32),
            VMEM((nt + 1, rows, 128), jnp.float32),
            VMEM((nt, rows, 128), jnp.float32),
            pltpu.SemaphoreType.DMA((ns + nt,)),
            pltpu.SemaphoreType.DMA((ns + nt,)),
        ],
        compiler_params=pltpu.CompilerParams(collective_id=1, has_side_effects=True),
        name="last_rows",
    )(chosen, gain.reshape(1, part))


def log_softmax(logits):
    seq_stages, tp_stages = bits_of("seq"), bits_of("tp")
    stages = tp_stages + seq_stages
    rows, part = logits.shape

    def kernel(logits_ref, out_ref, held, got, st_held, st_got, send_sem, recv_sem):
        greet(stages)
        held[0] = logits_ref[...]
        count = len(tp_stages)
        for k, stage in enumerate(tp_stages):
            swap(held.at[k], got.at[k], send_sem.at[k], recv_sem.at[k], stage).wait()
            held[k + 1] = held[k] + got[k]
        total = held[count]
        peak = jnp.max(total, -1, keepdims=True)
        mass = jnp.sum(jnp.exp(total - peak), -1, keepdims=True)
        st_held[0, :, :128] = jnp.broadcast_to(peak, (rows, 128))
        st_held[0, :, 128:] = jnp.broadcast_to(mass, (rows, 128))
        for k, stage in enumerate(seq_stages):
            n = count + k
            swap(st_held.at[k], st_got.at[k], send_sem.at[n], recv_sem.at[n], stage).wait()
            mine, theirs = st_held[k, :, :128], st_got[k, :, :128]
            top = jnp.maximum(mine, theirs)
            st_held[k + 1, :, :128] = top
            st_held[k + 1, :, 128:] = st_held[k, :, 128:] * jnp.exp(mine - top) + st_got[
                k, :, 128:
            ] * jnp.exp(theirs - top)
        last = len(seq_stages)
        out_ref[...] = total - st_held[last, :, :1] - jnp.log(st_held[last, :, 128:129])

    ns, nt = len(seq_stages), len(tp_stages)
    return pl.pallas_call(
        kernel,
        out_shape=jax.ShapeDtypeStruct((rows, part), jnp.float32),
        in_specs=[pl.BlockSpec(memory_space=VMEM)],
        out_specs=pl.BlockSpec(memory_space=VMEM),
        scratch_shapes=[
            VMEM((nt + 1, rows, part), jnp.float32),
            VMEM((nt, rows, part), jnp.float32),
            VMEM((ns + 1, rows, 256), jnp.float32),
            VMEM((ns, rows, 256), jnp.float32),
            pltpu.SemaphoreType.DMA((ns + nt,)),
            pltpu.SemaphoreType.DMA((ns + nt,)),
        ],
        compiler_params=pltpu.CompilerParams(collective_id=2, has_side_effects=True),
        name="log_softmax",
    )(logits)


def gather_columns(block):
    stages = bits_of("tp")
    rows, part = block.shape
    count = lax.axis_size("tp")

    def kernel(block_ref, out_ref, send_sem, recv_sem):
        greet(stages)
        me = lax.axis_index("tp")
        out_ref[:, pl.ds(pl.multiple_of(me * part, part), part)] = block_ref[...]
        for k, stage in enumerate(stages):
            wide = part << k
            start = pl.multiple_of((me // (1 << k)) * wide, wide)
            piece = out_ref.at[:, pl.ds(start, wide)]
            swap(piece, piece, send_sem.at[k], recv_sem.at[k], stage).wait()

    return pl.pallas_call(
        kernel,
        out_shape=jax.ShapeDtypeStruct((rows, part * count), block.dtype),
        in_specs=[pl.BlockSpec(memory_space=VMEM)],
        out_specs=pl.BlockSpec(memory_space=VMEM),
        scratch_shapes=[pltpu.SemaphoreType.DMA((len(stages),))] * 2,
        compiler_params=pltpu.CompilerParams(collective_id=3, has_side_effects=True),
        name="gather_columns",
    )(block)


def sum_over_tp(block):
    stages = bits_of("tp")
    rows, part = block.shape

    def kernel(block_ref, out_ref, held, got, send_sem, recv_sem):
        greet(stages)
        for k, stage in enumerate(stages):
            source = block_ref if k == 0 else held.at[k]
            swap(source, got.at[k], send_sem.at[k], recv_sem.at[k], stage).wait()
            total = source[...].astype(jnp.float32) + got[k].astype(jnp.float32)
            if k + 1 < len(stages):
                held[k + 1] = total.astype(jnp.bfloat16)
            else:
                out_ref[...] = total

    count = len(stages)
    return pl.pallas_call(
        kernel,
        out_shape=jax.ShapeDtypeStruct((rows, part), jnp.float32),
        in_specs=[pl.BlockSpec(memory_space=VMEM)],
        out_specs=pl.BlockSpec(memory_space=VMEM),
        scratch_shapes=[
            VMEM((count, rows, part), jnp.bfloat16),
            VMEM((count, rows, part), jnp.bfloat16),
            pltpu.SemaphoreType.DMA((count,)),
            pltpu.SemaphoreType.DMA((count,)),
        ],
        compiler_params=pltpu.CompilerParams(collective_id=4, has_side_effects=True),
        name="sum_over_tp",
    )(block)


def on_device(
    tokens,
    attn_gain,
    w_query,
    w_key,
    w_value,
    w_out,
    prefix_keys,
    prefix_values,
    shard_group,
    request_group,
    lengths,
    moe_gain,
    w_router,
    w_gate,
    w_up,
    w_down,
    routes,
    final_gain,
    w_head,
):
    f32 = jnp.float32
    bf16 = jnp.bfloat16
    seq_index = lax.axis_index("seq")
    tp_index = lax.axis_index("tp")
    seq_count = lax.axis_size("seq")
    tp_count = lax.axis_size("tp")
    tok_dev = tokens.shape[0]
    width_part = tokens.shape[1]
    shard_rows = prefix_keys.shape[0]
    prefix_length = shard_rows * seq_count // 2
    full_x = gather_columns(tokens)
    width = full_x.shape[1]
    normed = normalize(full_x.astype(f32), attn_gain).astype(bf16)
    heads = w_query.shape[1] // HD
    ends = jnp.cumsum(lengths)
    starts = ends - lengths
    local_index = seq_index * tok_dev + jnp.arange(tok_dev)
    own_request = request_of(local_index, ends)
    own_start = lookup(own_request, starts)
    own_group = lookup(own_request, request_group)
    position = (prefix_length + local_index - own_start).astype(f32)
    query = rotate(
        jnp.dot(normed, w_query, preferred_element_type=f32).reshape(tok_dev, heads, HD), position
    ).astype(bf16)
    key_rows = rotate(
        jnp.dot(normed, w_key, preferred_element_type=f32).reshape(tok_dev, heads, HD), position
    ).astype(bf16)
    key_rows = key_rows.reshape(tok_dev, heads * HD)
    value_rows = jnp.dot(normed, w_value, preferred_element_type=f32).astype(bf16)
    start_state = (
        jnp.full((heads, tok_dev), NEGATIVE, f32),
        jnp.zeros((heads, tok_dev), f32),
        jnp.zeros((heads, tok_dev, HD), f32),
    )
    pieces = (
        lax.all_gather(prefix_keys, "seq", axis=0, tiled=True),
        lax.all_gather(prefix_values, "seq", axis=0, tiled=True),
    )
    count = pieces[0].shape[0]
    shard_ids = jnp.arange(count) // shard_rows
    key_group = lookup(shard_ids, shard_group)
    fold_allowed = own_group[:, None] == key_group[None, :]
    state = attend(start_state, query, pieces[0], pieces[1], fold_allowed)
    own_allowed = (own_request[:, None] == own_request[None, :]) & (
        local_index[None, :] <= local_index[:, None]
    )
    state = attend(state, query, key_rows, value_rows, own_allowed)
    both_rows = jnp.concatenate([key_rows, value_rows], 1)
    behind = [from_behind(both_rows, "seq", step) for step in range(1, SPAN + 1)]
    half = heads * HD
    for step in range(1, SPAN + 1):
        moving = behind[step - 1]
        key_index = (seq_index - step) * tok_dev + jnp.arange(tok_dev)
        key_request = request_of(key_index, ends)
        allowed = (key_index >= 0)[None, :] & (own_request[:, None] == key_request[None, :])
        state = attend(state, query, moving[:, :half], moving[:, half:], allowed)
    best, total, accum = state
    attended = (accum / total[..., None]).astype(bf16)
    attended = jnp.transpose(attended, (1, 0, 2)).reshape(tok_dev, heads * HD)
    mixed = jnp.dot(attended, w_out, preferred_element_type=f32).astype(bf16)
    resid_full = (full_x.astype(f32) + sum_over_tp(mixed)).astype(bf16)
    moe_in = normalize(resid_full.astype(f32), moe_gain).astype(bf16)
    resid = lax.dynamic_slice_in_dim(resid_full, tp_index * width_part, width_part, 1)
    experts = w_router.shape[1]
    topk = routes.shape[1]
    probs = jax.nn.softmax(jnp.dot(moe_in, w_router, preferred_element_type=f32), -1)
    if 2 * topk >= experts:
        named = routes[:, :, None] == jnp.arange(experts)[None, None, :]
        share = jnp.sum(jnp.where(named, probs[:, None, :], 0.0), 1)
        shares = lax.all_gather(share, "seq", axis=0, tiled=True)
        own_share = lax.dynamic_slice_in_dim(shares, seq_index, 1, 1)
        rows = lax.all_gather(moe_in, "seq", axis=0, tiled=True)
        gate = jnp.dot(rows, w_gate[0], preferred_element_type=f32)
        up = jnp.dot(rows, w_up[0], preferred_element_type=f32)
        act = (jax.nn.silu(gate) * up).astype(bf16)
        partial_out = (jnp.dot(act, w_down[0], preferred_element_type=f32) * own_share).astype(bf16)
        summed = lax.psum_scatter(partial_out, "seq", scatter_dimension=0, tiled=True)
        moe_part = lax.psum_scatter(summed, "tp", scatter_dimension=1, tiled=True).astype(f32)
    else:
        flat = routes.reshape(-1)
        hits = (flat[:, None] == jnp.arange(experts)[None, :]).astype(jnp.int32)
        rank = jnp.sum((jnp.cumsum(hits, 0) - hits) * hits, 1)
        capacity = min(tok_dev, tp_count * max(1, 3 * tok_dev * topk // (2 * experts * tp_count)))
        target = flat * capacity + rank
        route_weight = jnp.sum(hits.reshape(tok_dev, topk, experts).astype(f32) * probs[:, None, :], -1)
        repeated = jnp.repeat(moe_in, topk, axis=0)
        outgoing = (
            jnp.zeros((experts * capacity, width), bf16)
            .at[target]
            .set(repeated)
            .reshape(experts, capacity, width)
        )
        arrived = lax.all_to_all(outgoing, "seq", split_axis=0, concat_axis=0, tiled=True)
        sources = arrived.shape[0]
        count = arrived.shape[1]
        rows = arrived.reshape(sources * count, width)
        gate = jnp.dot(rows, w_gate[0], preferred_element_type=f32)
        up = jnp.dot(rows, w_up[0], preferred_element_type=f32)
        act = (jax.nn.silu(gate) * up).astype(bf16)
        partial_out = jnp.dot(act, w_down[0], preferred_element_type=f32).reshape(sources, count, width)
        summed = lax.psum_scatter(partial_out, "tp", scatter_dimension=2, tiled=True).astype(bf16)
        returned = lax.all_to_all(summed, "seq", split_axis=0, concat_axis=0, tiled=True)
        picked = returned.reshape(experts * capacity, width_part)[target].reshape(
            tok_dev, topk, width_part
        )
        moe_part = jnp.sum(picked.astype(f32) * route_weight[:, :, None], 1)
    hidden = (resid.astype(f32) + moe_part).astype(bf16)
    last_hit = ((ends - 1)[:, None] == local_index[None, :]).astype(bf16)
    chosen = jnp.dot(last_hit, hidden, preferred_element_type=f32)
    final = last_rows(chosen, final_gain, width)
    log_probs = log_softmax(jnp.dot(final, w_head, preferred_element_type=f32))
    return (hidden, log_probs)


def solution(mesh):
    in_specs = (
        P("seq", "tp"),
        P(),
        P(None, "tp"),
        P(None, "tp"),
        P(None, "tp"),
        P("tp", None),
        P("seq", "tp"),
        P("seq", "tp"),
        P(),
        P(),
        P(),
        P(),
        P(),
        P("seq", None, "tp"),
        P("seq", None, "tp"),
        P("seq", "tp", None),
        P("seq", None),
        P("tp"),
        P("tp", "seq"),
    )
    out_specs = (P("seq", "tp"), P(None, "seq"))
    return jax.shard_map(
        on_device, mesh=mesh, in_specs=in_specs, out_specs=out_specs, check_vma=False
    )
```

```python
import jax
import jax.numpy as jnp
from jax import lax
from jax.experimental import pallas as pl
from jax.experimental.pallas import tpu as pltpu
from jax.sharding import PartitionSpec as P

HD = 128
SPAN = 4
VMEM = pltpu.VMEM


EPS = 1e-05
NEGATIVE = -1e30


def from_behind(value, axis, steps):
    count = lax.axis_size(axis)
    leading, last = (max(0, -steps), min(count, count - steps))
    return lax.ppermute(value, axis, [(source, source + steps) for source in range(leading, last)])


def normalize(rows, gain):
    inv = lax.rsqrt(jnp.mean(rows * rows, -1, keepdims=True) + EPS)
    return rows * inv * gain.astype(jnp.float32)


def rotate(vectors, position):
    half = vectors.shape[-1] // 2
    freq = 10000.0 ** (-jnp.arange(half).astype(jnp.float32) / half)
    angle = position[:, None] * freq[None, :]
    cosine = jnp.cos(angle)[:, None, :]
    sine = jnp.sin(angle)[:, None, :]
    first = vectors[..., :half]
    second = vectors[..., half:]
    return jnp.concatenate([first * cosine - second * sine, second * cosine + first * sine], -1)


def request_of(index, ends):
    return jnp.sum((index[:, None] >= ends[None, :]).astype(jnp.int32), 1)


def lookup(selector, table):
    hit = selector[:, None] == jnp.arange(table.shape[0])[None, :]
    return jnp.sum(jnp.where(hit, table[None, :], 0), 1)


def partner(axis, bit):
    index = lax.axis_index(axis)
    span = 1 << bit
    other = index + span - 2 * span * ((index // span) % 2)
    return {axis: other}


def greet(stages):
    barrier = pltpu.get_barrier_semaphore()
    for axis, bit in stages:
        pl.semaphore_signal(barrier, inc=1, device_id=partner(axis, bit))
    pl.semaphore_wait(barrier, len(stages))


def swap(source, target, send_sem, recv_sem, stage):
    copy = pltpu.make_async_remote_copy(
        src_ref=source, dst_ref=target, send_sem=send_sem, recv_sem=recv_sem,
        device_id=partner(*stage),
    )
    copy.start()
    return copy


def bits_of(axis):
    return [(axis, bit) for bit in range(lax.axis_size(axis).bit_length() - 1)]


def last_rows(chosen, gain, width):
    seq_stages, tp_stages = bits_of("seq"), bits_of("tp")
    stages = seq_stages + tp_stages
    rows, part = chosen.shape

    def kernel(chosen_ref, gain_ref, out_ref, held, got, sq_held, sq_got, send_sem, recv_sem):
        greet(stages)
        held[0] = chosen_ref[...]
        count = len(seq_stages)
        for k, stage in enumerate(seq_stages):
            swap(held.at[k], got.at[k], send_sem.at[k], recv_sem.at[k], stage).wait()
            held[k + 1] = held[k] + got[k]
        total = held[count]
        sq_held[0] = jnp.broadcast_to(jnp.sum(total * total, -1, keepdims=True), (rows, 128))
        for k, stage in enumerate(tp_stages):
            n = count + k
            swap(sq_held.at[k], sq_got.at[k], send_sem.at[n], recv_sem.at[n], stage).wait()
            sq_held[k + 1] = sq_held[k] + sq_got[k]
        square = sq_held[len(tp_stages)][:, :1]
        scaled = total * lax.rsqrt(square / width + EPS) * gain_ref[...].astype(jnp.float32)
        out_ref[...] = scaled.astype(jnp.bfloat16)

    ns, nt = len(seq_stages), len(tp_stages)
    return pl.pallas_call(
        kernel,
        out_shape=jax.ShapeDtypeStruct((rows, part), jnp.bfloat16),
        in_specs=[pl.BlockSpec(memory_space=VMEM)] * 2,
        out_specs=pl.BlockSpec(memory_space=VMEM),
        scratch_shapes=[
            VMEM((ns + 1, rows, part), jnp.float32),
            VMEM((ns, rows, part), jnp.float32),
            VMEM((nt + 1, rows, 128), jnp.float32),
            VMEM((nt, rows, 128), jnp.float32),
            pltpu.SemaphoreType.DMA((ns + nt,)),
            pltpu.SemaphoreType.DMA((ns + nt,)),
        ],
        compiler_params=pltpu.CompilerParams(collective_id=1, has_side_effects=True),
        name="last_rows",
    )(chosen, gain.reshape(1, part))


def log_softmax(logits):
    seq_stages, tp_stages = bits_of("seq"), bits_of("tp")
    stages = tp_stages + seq_stages
    rows, part = logits.shape

    def kernel(logits_ref, out_ref, held, got, st_held, st_got, send_sem, recv_sem):
        greet(stages)
        held[0] = logits_ref[...]
        count = len(tp_stages)
        for k, stage in enumerate(tp_stages):
            swap(held.at[k], got.at[k], send_sem.at[k], recv_sem.at[k], stage).wait()
            held[k + 1] = held[k] + got[k]
        total = held[count]
        peak = jnp.max(total, -1, keepdims=True)
        mass = jnp.sum(jnp.exp(total - peak), -1, keepdims=True)
        st_held[0, :, :128] = jnp.broadcast_to(peak, (rows, 128))
        st_held[0, :, 128:] = jnp.broadcast_to(mass, (rows, 128))
        for k, stage in enumerate(seq_stages):
            n = count + k
            swap(st_held.at[k], st_got.at[k], send_sem.at[n], recv_sem.at[n], stage).wait()
            mine, theirs = st_held[k, :, :128], st_got[k, :, :128]
            top = jnp.maximum(mine, theirs)
            st_held[k + 1, :, :128] = top
            st_held[k + 1, :, 128:] = st_held[k, :, 128:] * jnp.exp(mine - top) + st_got[
                k, :, 128:
            ] * jnp.exp(theirs - top)
        last = len(seq_stages)
        out_ref[...] = total - st_held[last, :, :1] - jnp.log(st_held[last, :, 128:129])

    ns, nt = len(seq_stages), len(tp_stages)
    return pl.pallas_call(
        kernel,
        out_shape=jax.ShapeDtypeStruct((rows, part), jnp.float32),
        in_specs=[pl.BlockSpec(memory_space=VMEM)],
        out_specs=pl.BlockSpec(memory_space=VMEM),
        scratch_shapes=[
            VMEM((nt + 1, rows, part), jnp.float32),
            VMEM((nt, rows, part), jnp.float32),
            VMEM((ns + 1, rows, 256), jnp.float32),
            VMEM((ns, rows, 256), jnp.float32),
            pltpu.SemaphoreType.DMA((ns + nt,)),
            pltpu.SemaphoreType.DMA((ns + nt,)),
        ],
        compiler_params=pltpu.CompilerParams(collective_id=2, has_side_effects=True),
        name="log_softmax",
    )(logits)


def gather_columns(block):
    stages = bits_of("tp")
    rows, part = block.shape
    count = lax.axis_size("tp")

    def kernel(block_ref, out_ref, send_sem, recv_sem):
        greet(stages)
        me = lax.axis_index("tp")
        out_ref[:, pl.ds(pl.multiple_of(me * part, part), part)] = block_ref[...]
        for k, stage in enumerate(stages):
            wide = part << k
            start = pl.multiple_of((me // (1 << k)) * wide, wide)
            piece = out_ref.at[:, pl.ds(start, wide)]
            swap(piece, piece, send_sem.at[k], recv_sem.at[k], stage).wait()

    return pl.pallas_call(
        kernel,
        out_shape=jax.ShapeDtypeStruct((rows, part * count), block.dtype),
        in_specs=[pl.BlockSpec(memory_space=VMEM)],
        out_specs=pl.BlockSpec(memory_space=VMEM),
        scratch_shapes=[pltpu.SemaphoreType.DMA((len(stages),))] * 2,
        compiler_params=pltpu.CompilerParams(collective_id=3, has_side_effects=True),
        name="gather_columns",
    )(block)


def sum_over_tp(block):
    stages = bits_of("tp")
    rows, part = block.shape

    def kernel(block_ref, out_ref, held, got, send_sem, recv_sem):
        greet(stages)
        for k, stage in enumerate(stages):
            source = block_ref if k == 0 else held.at[k]
            swap(source, got.at[k], send_sem.at[k], recv_sem.at[k], stage).wait()
            total = source[...].astype(jnp.float32) + got[k].astype(jnp.float32)
            if k + 1 < len(stages):
                held[k + 1] = total.astype(jnp.bfloat16)
            else:
                out_ref[...] = total

    count = len(stages)
    return pl.pallas_call(
        kernel,
        out_shape=jax.ShapeDtypeStruct((rows, part), jnp.float32),
        in_specs=[pl.BlockSpec(memory_space=VMEM)],
        out_specs=pl.BlockSpec(memory_space=VMEM),
        scratch_shapes=[
            VMEM((count, rows, part), jnp.bfloat16),
            VMEM((count, rows, part), jnp.bfloat16),
            pltpu.SemaphoreType.DMA((count,)),
            pltpu.SemaphoreType.DMA((count,)),
        ],
        compiler_params=pltpu.CompilerParams(collective_id=4, has_side_effects=True),
        name="sum_over_tp",
    )(block)


def bit(index, place):
    return (index // (1 << place)) % 2


def reversed_index(count):
    me = lax.axis_index("seq")
    return sum(bit(me, k) * (1 << (count - 1 - k)) for k in range(count))


def advance(chains):
    for turn in range(max(len(chain) for chain in chains)):
        for chain in chains:
            if turn < len(chain):
                chain[turn]()


def spread_rows(rows, share):
    count = lax.axis_size("seq").bit_length() - 1
    blocks = 1 << count
    tall, wide = rows.shape
    quarter = wide // 4
    experts = share.shape[0]
    stages = bits_of("seq") + bits_of("tp")
    slots = 4 * count + 1

    def kernel(rows_ref, share_ref, out_ref, share_out, send_sem, recv_sem):
        place = reversed_index(count)
        tp = lax.axis_index("tp")
        out_ref[place] = rows_ref[...]
        share_out[place] = share_ref[...]
        greet(stages)
        used = iter(range(slots))
        flying = {}

        def hop(name, stage, view):
            def act():
                if name in flying:
                    flying[name].wait()
                slot = next(used)
                piece = view()
                flying[name] = swap(piece, piece, send_sem.at[slot], recv_sem.at[slot], stage)

            return act

        def span_of(j):
            return pl.ds((place // (1 << j)) * (1 << j), 1 << j)

        def rows_view(j, start, size):
            return lambda: out_ref.at[span_of(j), :, pl.ds(start, size)]

        own = pl.multiple_of(tp * quarter, quarter)
        crossing = [
            hop("q", ("seq", count - 1 - j), rows_view(j, own, quarter)) for j in range(count - 1)
        ]
        crossing.append(hop("q", ("tp", 0), rows_view(count - 1, own, quarter)))
        crossing.append(hop("q", ("seq", 0), rows_view(count - 1, 0, 2 * quarter)))
        chains = [crossing]
        for part in (2, 3):
            chains.append([
                hop(part, ("seq", count - 1 - j), rows_view(j, part * quarter, quarter))
                for j in range(count)
            ])
        chains.append([
            hop("s", ("seq", count - 1 - j), lambda j=j: share_out.at[span_of(j)])
            for j in range(count)
        ])
        advance(chains)
        for copy in flying.values():
            copy.wait()

    return pl.pallas_call(
        kernel,
        out_shape=(
            jax.ShapeDtypeStruct((blocks, tall, wide), rows.dtype),
            jax.ShapeDtypeStruct((blocks, experts, tall), share.dtype),
        ),
        in_specs=[pl.BlockSpec(memory_space=VMEM)] * 2,
        out_specs=(pl.BlockSpec(memory_space=VMEM), pl.BlockSpec(memory_space=VMEM)),
        scratch_shapes=[pltpu.SemaphoreType.DMA((slots,)), pltpu.SemaphoreType.DMA((slots,))],
        compiler_params=pltpu.CompilerParams(
            collective_id=5, has_side_effects=True, vmem_limit_bytes=40 << 20
        ),
        name="spread_rows",
    )(rows, share)


def collect_rows(partial):
    blocks, tall, wide = partial.shape
    count = blocks.bit_length() - 1
    half = wide // 2
    groups = 4
    w = half // groups
    stages = bits_of("seq") + bits_of("tp")
    slots = groups * (2 * count + 1)

    def kernel(part_ref, out_ref, *rest):
        buffers, (send_sem, recv_sem) = iter(rest[:-2]), rest[-2:]
        greet(stages)
        me, tp = lax.axis_index("seq"), lax.axis_index("tp")
        used = iter(range(slots))

        def send(source, target, stage):
            slot = next(used)
            return swap(source, target, send_sem.at[slot], recv_sem.at[slot], stage)

        def add(size, mine, base, got, out):
            def body(i, _):
                total = mine[base + i].astype(jnp.float32) + got[i].astype(jnp.float32)
                out[i] = total.astype(jnp.bfloat16)
                return 0

            lax.fori_loop(0, size, body, 0)

        def scatter(state, j):
            size = 1 << (count - 1 - j)
            got, out = next(buffers), next(buffers)
            mine = bit(me, j)
            source = state
            copy = send(source.at[pl.ds((1 - mine) * size, size)], got, ("seq", j))

            def end():
                copy.wait()
                add(size, source, mine * size, got, out)
                return out

            return end

        def straight(group):
            ends, states = {}, {}
            views = [part_ref.at[:, :, pl.ds(h * half + group * w, w)] for h in range(2)]

            def step(j):
                def act():
                    for h in range(2):
                        state = views[h] if j == 0 else ends[h]()
                        ends[h] = scatter(state, j)

                return act

            def cross():
                both, got = next(buffers), next(buffers)
                for h in range(2):
                    both[h] = ends[h]()[0]
                states["both"], states["got"] = both, got
                states["copy"] = send(both.at[1 - tp], got, ("tp", 0))

            def finish():
                states["copy"].wait()
                out_ref[:, group * w : (group + 1) * w] = states["both"][tp].astype(
                    jnp.float32
                ) + states["got"][...].astype(jnp.float32)

            return [step(j) for j in range(count)] + [cross, finish]

        def crossing(group):
            ends, states = {}, {}
            size = blocks // 2

            def first():
                for h in range(2):
                    got = next(buffers)
                    mine = bit(me, 0)
                    view = part_ref.at[:, :, pl.ds(h * half + group * w, w)]
                    copy = send(view.at[pl.ds((1 - mine) * size, size)], got, ("seq", 0))
                    states[h] = (view, mine, got, copy)
                states["both"] = next(buffers)

            def cross():
                both, got = states["both"], next(buffers)
                for h in range(2):
                    view, mine, landed, copy = states[h]
                    copy.wait()
                    add(size, view, mine * size, landed, both.at[h])
                states["got"] = got
                states["copy"] = send(both.at[1 - tp], got, ("tp", 0))

            def second():
                states["copy"].wait()
                out = next(buffers)
                add(size, states["both"].at[tp], 0, states["got"], out)
                ends[0] = scatter(out, 1)

            def step(j):
                def act():
                    ends[0] = scatter(ends[0](), j)

                return act

            def finish():
                out_ref[:, group * w : (group + 1) * w] = ends[0]()[0].astype(jnp.float32)

            return [first, cross, second] + [step(j) for j in range(2, count)] + [finish]

        advance([crossing(g) if g < groups // 2 else straight(g) for g in range(groups)])

    def shapes():
        bf16 = jnp.bfloat16
        listing = []

        def scatter(j):
            size = 1 << (count - 1 - j)
            listing.extend([VMEM((size, tall, w), bf16)] * 2)

        def straight():
            cross = [VMEM((2, tall, w), bf16), VMEM((tall, w), bf16)]
            return [lambda j=j: (scatter(j), scatter(j)) for j in range(count)] + [
                lambda: listing.extend(cross), lambda: None
            ]

        def crossing():
            size = blocks // 2
            block = VMEM((size, tall, w), bf16)
            pair = VMEM((2, size, tall, w), bf16)
            return [
                lambda: listing.extend([block, block, pair]),
                lambda: listing.extend([block]),
                lambda: (listing.extend([block]), scatter(1)),
            ] + [lambda j=j: scatter(j) for j in range(2, count)] + [lambda: None]

        advance([crossing() if g < groups // 2 else straight() for g in range(groups)])
        return listing

    return pl.pallas_call(
        kernel,
        out_shape=jax.ShapeDtypeStruct((tall, half), jnp.float32),
        in_specs=[pl.BlockSpec(memory_space=VMEM)],
        out_specs=pl.BlockSpec(memory_space=VMEM),
        scratch_shapes=shapes()
        + [pltpu.SemaphoreType.DMA((slots,)), pltpu.SemaphoreType.DMA((slots,))],
        compiler_params=pltpu.CompilerParams(
            collective_id=6, has_side_effects=True, vmem_limit_bytes=56 << 20
        ),
        name="collect_rows",
    )(partial)


def attention(query, prefix_keys, prefix_values, suffix, bias):
    tall, wide = query.shape
    heads = wide // HD
    cached = prefix_keys.shape[0]
    keys = bias.shape[1]
    many = len(suffix)
    scale = HD ** (-0.5)

    def kernel(query_ref, cached_k, cached_v, bias_ref, *rest):
        suffix_k, suffix_v, out_ref = rest[:many], rest[many : 2 * many], rest[2 * many]
        head = query_ref[...]
        scores = [
            lax.dot_general(
                head, block[...], (((1,), (1,)), ((), ())), preferred_element_type=jnp.float32
            )
            for block in (cached_k, *suffix_k)
        ]
        scores = jnp.concatenate(scores, 1) * scale + bias_ref[...]
        weights = jnp.exp(scores - jnp.max(scores, -1, keepdims=True))
        total = jnp.sum(weights, -1, keepdims=True)
        weights = weights.astype(jnp.bfloat16)
        summed = jnp.dot(weights[:, :cached], cached_v[...], preferred_element_type=jnp.float32)
        for n, block in enumerate(suffix_v):
            start = cached + n * tall
            summed += jnp.dot(
                weights[:, start : start + tall], block[...], preferred_element_type=jnp.float32
            )
        out_ref[...] = (summed / total).astype(jnp.bfloat16)

    def column(rows, offset):
        return pl.BlockSpec((rows, HD), lambda h: (0, h + offset))

    return pl.pallas_call(
        kernel,
        out_shape=jax.ShapeDtypeStruct((tall, wide), jnp.bfloat16),
        grid=(heads,),
        in_specs=[column(tall, 0), column(cached, 0), column(cached, 0)]
        + [pl.BlockSpec((tall, keys), lambda h: (0, 0))]
        + [column(tall, 0)] * many
        + [column(tall, heads)] * many,
        out_specs=column(tall, 0),
        cost_estimate=pl.CostEstimate(
            flops=4 * tall * keys * wide, bytes_accessed=4 * keys * wide, transcendentals=0
        ),
        name="attention",
    )(query, prefix_keys, prefix_values, bias, *suffix, *suffix)


def on_device(
    tokens,
    attn_gain,
    w_query,
    w_key,
    w_value,
    w_out,
    prefix_keys,
    prefix_values,
    shard_group,
    request_group,
    lengths,
    moe_gain,
    w_router,
    w_gate,
    w_up,
    w_down,
    routes,
    final_gain,
    w_head,
):
    f32 = jnp.float32
    bf16 = jnp.bfloat16
    seq_index = lax.axis_index("seq")
    tp_index = lax.axis_index("tp")
    seq_count = lax.axis_size("seq")
    tp_count = lax.axis_size("tp")
    tok_dev = tokens.shape[0]
    width_part = tokens.shape[1]
    shard_rows = prefix_keys.shape[0]
    prefix_length = shard_rows * seq_count // 2
    full_x = gather_columns(tokens)
    width = full_x.shape[1]
    normed = normalize(full_x.astype(f32), attn_gain).astype(bf16)
    heads = w_query.shape[1] // HD
    ends = jnp.cumsum(lengths)
    starts = ends - lengths
    local_index = seq_index * tok_dev + jnp.arange(tok_dev)
    own_request = request_of(local_index, ends)
    own_start = lookup(own_request, starts)
    own_group = lookup(own_request, request_group)
    position = (prefix_length + local_index - own_start).astype(f32)
    query = rotate(
        jnp.dot(normed, w_query, preferred_element_type=f32).reshape(tok_dev, heads, HD), position
    ).astype(bf16)
    key_rows = rotate(
        jnp.dot(normed, w_key, preferred_element_type=f32).reshape(tok_dev, heads, HD), position
    ).astype(bf16)
    key_rows = key_rows.reshape(tok_dev, heads * HD)
    value_rows = jnp.dot(normed, w_value, preferred_element_type=f32).astype(bf16)
    pieces = (
        lax.all_gather(prefix_keys, "seq", axis=0, tiled=True),
        lax.all_gather(prefix_values, "seq", axis=0, tiled=True),
    )
    count = pieces[0].shape[0]
    shard_ids = jnp.arange(count) // shard_rows
    key_group = lookup(shard_ids, shard_group)
    fold_allowed = own_group[:, None] == key_group[None, :]
    own_allowed = (own_request[:, None] == own_request[None, :]) & (
        local_index[None, :] <= local_index[:, None]
    )
    both_rows = jnp.concatenate([key_rows, value_rows], 1)
    suffix = [both_rows] + [from_behind(both_rows, "seq", step) for step in range(1, SPAN + 1)]
    permitted = [fold_allowed, own_allowed]
    for step in range(1, SPAN + 1):
        key_index = (seq_index - step) * tok_dev + jnp.arange(tok_dev)
        key_request = request_of(key_index, ends)
        permitted.append(
            (key_index >= 0)[None, :] & (own_request[:, None] == key_request[None, :])
        )
    bias = jnp.where(jnp.concatenate(permitted, 1), 0.0, NEGATIVE)
    attended = attention(query.reshape(tok_dev, heads * HD), *pieces, suffix, bias)
    mixed = jnp.dot(attended, w_out, preferred_element_type=f32).astype(bf16)
    resid_full = (full_x.astype(f32) + sum_over_tp(mixed)).astype(bf16)
    moe_in = normalize(resid_full.astype(f32), moe_gain).astype(bf16)
    resid = lax.dynamic_slice_in_dim(resid_full, tp_index * width_part, width_part, 1)
    experts = w_router.shape[1]
    topk = routes.shape[1]
    probs = jax.nn.softmax(jnp.dot(moe_in, w_router, preferred_element_type=f32), -1)
    if 2 * topk >= experts and tp_count == 2:
        named = routes[:, :, None] == jnp.arange(experts)[None, None, :]
        share = jnp.sum(jnp.where(named, probs[:, None, :], 0.0), 1)
        blocks, shares = spread_rows(moe_in, share.T)
        own_share = lax.dynamic_slice_in_dim(shares, seq_index, 1, 1).reshape(-1, 1)
        rows = blocks.reshape(-1, width)
        gate = jnp.dot(rows, w_gate[0], preferred_element_type=f32)
        up = jnp.dot(rows, w_up[0], preferred_element_type=f32)
        act = (jax.nn.silu(gate) * up).astype(bf16)
        partial_out = (jnp.dot(act, w_down[0], preferred_element_type=f32) * own_share).astype(bf16)
        moe_part = collect_rows(partial_out.reshape(seq_count, tok_dev, width))
    else:
        flat = routes.reshape(-1)
        hits = (flat[:, None] == jnp.arange(experts)[None, :]).astype(jnp.int32)
        rank = jnp.sum((jnp.cumsum(hits, 0) - hits) * hits, 1)
        capacity = min(tok_dev, tp_count * max(1, 3 * tok_dev * topk // (2 * experts * tp_count)))
        target = flat * capacity + rank
        route_weight = jnp.sum(hits.reshape(tok_dev, topk, experts).astype(f32) * probs[:, None, :], -1)
        repeated = jnp.repeat(moe_in, topk, axis=0)
        outgoing = (
            jnp.zeros((experts * capacity, width), bf16)
            .at[target]
            .set(repeated)
            .reshape(experts, capacity, width)
        )
        arrived = lax.all_to_all(outgoing, "seq", split_axis=0, concat_axis=0, tiled=True)
        sources = arrived.shape[0]
        count = arrived.shape[1]
        rows = arrived.reshape(sources * count, width)
        gate = jnp.dot(rows, w_gate[0], preferred_element_type=f32)
        up = jnp.dot(rows, w_up[0], preferred_element_type=f32)
        act = (jax.nn.silu(gate) * up).astype(bf16)
        partial_out = jnp.dot(act, w_down[0], preferred_element_type=f32).reshape(sources, count, width)
        summed = lax.psum_scatter(partial_out, "tp", scatter_dimension=2, tiled=True).astype(bf16)
        returned = lax.all_to_all(summed, "seq", split_axis=0, concat_axis=0, tiled=True)
        picked = returned.reshape(experts * capacity, width_part)[target].reshape(
            tok_dev, topk, width_part
        )
        moe_part = jnp.sum(picked.astype(f32) * route_weight[:, :, None], 1)
    hidden = (resid.astype(f32) + moe_part).astype(bf16)
    last_hit = ((ends - 1)[:, None] == local_index[None, :]).astype(bf16)
    chosen = jnp.dot(last_hit, hidden, preferred_element_type=f32)
    final = last_rows(chosen, final_gain, width)
    log_probs = log_softmax(jnp.dot(final, w_head, preferred_element_type=f32))
    return (hidden, log_probs)


def solution(mesh):
    in_specs = (
        P("seq", "tp"),
        P(),
        P(None, "tp"),
        P(None, "tp"),
        P(None, "tp"),
        P("tp", None),
        P("seq", "tp"),
        P("seq", "tp"),
        P(),
        P(),
        P(),
        P(),
        P(),
        P("seq", None, "tp"),
        P("seq", None, "tp"),
        P("seq", "tp", None),
        P("seq", None),
        P("tp"),
        P("tp", "seq"),
    )
    out_specs = (P("seq", "tp"), P(None, "seq"))
    return jax.shard_map(
        on_device, mesh=mesh, in_specs=in_specs, out_specs=out_specs, check_vma=False
    )
```

```python
import heapq
import jax
import jax.numpy as jnp
from jax import lax
from jax.experimental import pallas as pl
from jax.experimental.pallas import tpu as pltpu
from jax.sharding import PartitionSpec as P

HD = 128
SPAN = 4
VMEM = pltpu.VMEM


EPS = 1e-05
NEGATIVE = -1e30


def from_behind(value, axis, steps):
    count = lax.axis_size(axis)
    leading, last = (max(0, -steps), min(count, count - steps))
    return lax.ppermute(value, axis, [(source, source + steps) for source in range(leading, last)])


def normalize(rows, gain):
    inv = lax.rsqrt(jnp.mean(rows * rows, -1, keepdims=True) + EPS)
    return rows * inv * gain.astype(jnp.float32)


def rotate(vectors, position):
    half = vectors.shape[-1] // 2
    freq = 10000.0 ** (-jnp.arange(half).astype(jnp.float32) / half)
    angle = position[:, None] * freq[None, :]
    cosine = jnp.cos(angle)[:, None, :]
    sine = jnp.sin(angle)[:, None, :]
    first = vectors[..., :half]
    second = vectors[..., half:]
    return jnp.concatenate([first * cosine - second * sine, second * cosine + first * sine], -1)


def request_of(index, ends):
    return jnp.sum((index[:, None] >= ends[None, :]).astype(jnp.int32), 1)


def lookup(selector, table):
    hit = selector[:, None] == jnp.arange(table.shape[0])[None, :]
    return jnp.sum(jnp.where(hit, table[None, :], 0), 1)


def partner(axis, bit):
    index = lax.axis_index(axis)
    span = 1 << bit
    other = index + span - 2 * span * ((index // span) % 2)
    return {axis: other}


def greet(stages):
    barrier = pltpu.get_barrier_semaphore()
    for axis, bit in stages:
        pl.semaphore_signal(barrier, inc=1, device_id=partner(axis, bit))
    pl.semaphore_wait(barrier, len(stages))


def swap(source, target, send_sem, recv_sem, stage):
    copy = pltpu.make_async_remote_copy(
        src_ref=source, dst_ref=target, send_sem=send_sem, recv_sem=recv_sem,
        device_id=partner(*stage),
    )
    copy.start()
    return copy


def bits_of(axis):
    return [(axis, bit) for bit in range(lax.axis_size(axis).bit_length() - 1)]


def last_rows(chosen, gain, width):
    seq_stages, tp_stages = bits_of("seq"), bits_of("tp")
    stages = seq_stages + tp_stages
    rows, part = chosen.shape

    def kernel(chosen_ref, gain_ref, out_ref, held, got, sq_held, sq_got, send_sem, recv_sem):
        greet(stages)
        held[0] = chosen_ref[...]
        count = len(seq_stages)
        for k, stage in enumerate(seq_stages):
            swap(held.at[k], got.at[k], send_sem.at[k], recv_sem.at[k], stage).wait()
            held[k + 1] = held[k] + got[k]
        total = held[count]
        sq_held[0] = jnp.broadcast_to(jnp.sum(total * total, -1, keepdims=True), (rows, 128))
        for k, stage in enumerate(tp_stages):
            n = count + k
            swap(sq_held.at[k], sq_got.at[k], send_sem.at[n], recv_sem.at[n], stage).wait()
            sq_held[k + 1] = sq_held[k] + sq_got[k]
        square = sq_held[len(tp_stages)][:, :1]
        scaled = total * lax.rsqrt(square / width + EPS) * gain_ref[...].astype(jnp.float32)
        out_ref[...] = scaled.astype(jnp.bfloat16)

    ns, nt = len(seq_stages), len(tp_stages)
    return pl.pallas_call(
        kernel,
        out_shape=jax.ShapeDtypeStruct((rows, part), jnp.bfloat16),
        in_specs=[pl.BlockSpec(memory_space=VMEM)] * 2,
        out_specs=pl.BlockSpec(memory_space=VMEM),
        scratch_shapes=[
            VMEM((ns + 1, rows, part), jnp.float32),
            VMEM((ns, rows, part), jnp.float32),
            VMEM((nt + 1, rows, 128), jnp.float32),
            VMEM((nt, rows, 128), jnp.float32),
            pltpu.SemaphoreType.DMA((ns + nt,)),
            pltpu.SemaphoreType.DMA((ns + nt,)),
        ],
        compiler_params=pltpu.CompilerParams(collective_id=1, has_side_effects=True),
        name="last_rows",
    )(chosen, gain.reshape(1, part))


def log_softmax(logits):
    seq_stages, tp_stages = bits_of("seq"), bits_of("tp")
    stages = tp_stages + seq_stages
    rows, part = logits.shape

    def kernel(logits_ref, out_ref, held, got, st_held, st_got, send_sem, recv_sem):
        greet(stages)
        held[0] = logits_ref[...]
        count = len(tp_stages)
        for k, stage in enumerate(tp_stages):
            swap(held.at[k], got.at[k], send_sem.at[k], recv_sem.at[k], stage).wait()
            held[k + 1] = held[k] + got[k]
        total = held[count]
        peak = jnp.max(total, -1, keepdims=True)
        mass = jnp.sum(jnp.exp(total - peak), -1, keepdims=True)
        st_held[0, :, :128] = jnp.broadcast_to(peak, (rows, 128))
        st_held[0, :, 128:] = jnp.broadcast_to(mass, (rows, 128))
        for k, stage in enumerate(seq_stages):
            n = count + k
            swap(st_held.at[k], st_got.at[k], send_sem.at[n], recv_sem.at[n], stage).wait()
            mine, theirs = st_held[k, :, :128], st_got[k, :, :128]
            top = jnp.maximum(mine, theirs)
            st_held[k + 1, :, :128] = top
            st_held[k + 1, :, 128:] = st_held[k, :, 128:] * jnp.exp(mine - top) + st_got[
                k, :, 128:
            ] * jnp.exp(theirs - top)
        last = len(seq_stages)
        out_ref[...] = total - st_held[last, :, :1] - jnp.log(st_held[last, :, 128:129])

    ns, nt = len(seq_stages), len(tp_stages)
    return pl.pallas_call(
        kernel,
        out_shape=jax.ShapeDtypeStruct((rows, part), jnp.float32),
        in_specs=[pl.BlockSpec(memory_space=VMEM)],
        out_specs=pl.BlockSpec(memory_space=VMEM),
        scratch_shapes=[
            VMEM((nt + 1, rows, part), jnp.float32),
            VMEM((nt, rows, part), jnp.float32),
            VMEM((ns + 1, rows, 256), jnp.float32),
            VMEM((ns, rows, 256), jnp.float32),
            pltpu.SemaphoreType.DMA((ns + nt,)),
            pltpu.SemaphoreType.DMA((ns + nt,)),
        ],
        compiler_params=pltpu.CompilerParams(collective_id=2, has_side_effects=True),
        name="log_softmax",
    )(logits)


def gather_front(block, *cached):
    stages = bits_of("tp")
    rows, part = block.shape
    tp_count = lax.axis_size("tp")
    count = lax.axis_size("seq").bit_length() - 1
    many = len(cached)
    slots = many * count + len(stages)

    def kernel(block_ref, *rest):
        cached_refs, out_ref, outs = rest[:many], rest[many], rest[many + 1 : 2 * many + 1]
        send_sem, recv_sem = rest[-2:]
        me = lax.axis_index("tp")
        place = reversed_index(count)
        out_ref[:, pl.ds(pl.multiple_of(me * part, part), part)] = block_ref[...]
        for source, target in zip(cached_refs, outs):
            target[place] = source[...]
        greet(stages + bits_of("seq"))
        used = iter(range(slots))

        def send(piece, stage):
            slot = next(used)
            return swap(piece, piece, send_sem.at[slot], recv_sem.at[slot], stage)

        def tp_step(k, stage):
            wide = part << k
            start_at = pl.multiple_of((me // (1 << k)) * wide, wide)
            flying = []
            return (
                stage,
                4.0,
                lambda: flying.append(send(out_ref.at[:, pl.ds(start_at, wide)], stage)),
                lambda: flying[0].wait(),
            )

        chains = [[tp_step(k, stage) for k, stage in enumerate(stages)]]
        for target in outs:
            def view(j, _, target=target):
                return target.at[pl.ds((place // (1 << j)) * (1 << j), 1 << j)]

            chains.append(doubling(count, [], view, send))
        advance(chains)

    shapes = [jax.ShapeDtypeStruct((rows, part * tp_count), block.dtype)]
    for one in cached:
        shapes.append(jax.ShapeDtypeStruct((1 << count, *one.shape), one.dtype))
    return pl.pallas_call(
        kernel,
        out_shape=tuple(shapes),
        in_specs=[pl.BlockSpec(memory_space=VMEM)] * (1 + many),
        out_specs=tuple(pl.BlockSpec(memory_space=VMEM) for _ in shapes),
        scratch_shapes=[pltpu.SemaphoreType.DMA((slots,))] * 2,
        compiler_params=pltpu.CompilerParams(collective_id=3, has_side_effects=True),
        name="gather_front",
    )(block, *cached)


def sum_over_tp(block):
    stages = bits_of("tp")
    rows, part = block.shape

    def kernel(block_ref, out_ref, held, got, send_sem, recv_sem):
        greet(stages)
        for k, stage in enumerate(stages):
            source = block_ref if k == 0 else held.at[k]
            swap(source, got.at[k], send_sem.at[k], recv_sem.at[k], stage).wait()
            total = source[...].astype(jnp.float32) + got[k].astype(jnp.float32)
            if k + 1 < len(stages):
                held[k + 1] = total.astype(jnp.bfloat16)
            else:
                out_ref[...] = total

    count = len(stages)
    return pl.pallas_call(
        kernel,
        out_shape=jax.ShapeDtypeStruct((rows, part), jnp.float32),
        in_specs=[pl.BlockSpec(memory_space=VMEM)],
        out_specs=pl.BlockSpec(memory_space=VMEM),
        scratch_shapes=[
            VMEM((count, rows, part), jnp.bfloat16),
            VMEM((count, rows, part), jnp.bfloat16),
            pltpu.SemaphoreType.DMA((count,)),
            pltpu.SemaphoreType.DMA((count,)),
        ],
        compiler_params=pltpu.CompilerParams(collective_id=4, has_side_effects=True),
        name="sum_over_tp",
    )(block)


def bit(index, place):
    return (index // (1 << place)) % 2


def reversed_index(count):
    me = lax.axis_index("seq")
    return sum(bit(me, k) * (1 << (count - 1 - k)) for k in range(count))


def carrier(stage):
    axis, place = stage
    return {"tp": "y", "share": "s"}.get(axis) or "cxz"[min(place, 2)]


def advance(chains):
    left = [sum(step[1] for step in chain) for chain in chains]
    place, busy, events = [0] * len(chains), set(), []
    waiting, now = set(range(len(chains))), 0.0
    while waiting or events:
        for c in sorted(waiting, key=lambda c: (-left[c], c)):
            stage, cost, start, _ = chains[c][place[c]]
            if carrier(stage) not in busy:
                start()
                busy.add(carrier(stage))
                waiting.remove(c)
                heapq.heappush(events, (now + cost, c))
        now, c = heapq.heappop(events)
        stage, cost, _, end = chains[c][place[c]]
        end()
        busy.remove(carrier(stage))
        left[c] -= cost
        place[c] += 1
        if place[c] < len(chains[c]):
            waiting.add(c)


def doubling(count, axis_hops, view, send):
    steps = []
    plan = [(("seq", count - 1 - j), j, None) for j in range(count)]
    plan[count - 1 : count - 1] = axis_hops
    for stage, j, columns in plan:
        flying = []

        def start(stage=stage, j=j, columns=columns, flying=flying):
            flying.append(send(view(j, columns), stage))

        price = {"z": max(2.0, 1.0 * (1 << j)), "x": 1 << j, "y": 1 << j, "c": 0.3 * (1 << j)}[
            carrier(stage)
        ]
        steps.append((stage, price, start, lambda flying=flying: flying[0].wait()))
    return steps


def spread_rows(rows, share):
    count = lax.axis_size("seq").bit_length() - 1
    blocks = 1 << count
    tall, wide = rows.shape
    part = wide // 8
    experts = share.shape[0]
    stages = bits_of("seq") + bits_of("tp")
    slots = 7 * count + 2

    def kernel(rows_ref, share_ref, out_ref, share_out, send_sem, recv_sem):
        place = reversed_index(count)
        tp = lax.axis_index("tp")
        out_ref[place] = rows_ref[...]
        share_out[place] = share_ref[...]
        greet(stages)
        used = iter(range(slots))

        def send(piece, stage):
            slot = next(used)
            return swap(piece, piece, send_sem.at[slot], recv_sem.at[slot], stage)

        def span_of(j):
            return pl.ds((place // (1 << j)) * (1 << j), 1 << j)

        chains = []
        for n in range(2):
            base = 2 * n * part
            own = pl.multiple_of(base + tp * part, part)

            def view(j, columns, base=base, own=own):
                if columns is None and j == count - 1:
                    return out_ref.at[span_of(j), :, pl.ds(base, 2 * part)]
                return out_ref.at[span_of(j), :, pl.ds(own, part)]

            chains.append(doubling(count, [(("tp", 0), count - 1, "own")], view, send))
        for n in range(4, 8):
            chains.append(
                doubling(
                    count, [], lambda j, _, n=n: out_ref.at[span_of(j), :, pl.ds(n * part, part)], send
                )
            )
        small = doubling(count, [], lambda j, _: share_out.at[span_of(j)], send)
        chains.append([(("share", 0), cost, start, end) for _, cost, start, end in small])
        advance(chains)

    return pl.pallas_call(
        kernel,
        out_shape=(
            jax.ShapeDtypeStruct((blocks, tall, wide), rows.dtype),
            jax.ShapeDtypeStruct((blocks, experts, tall), share.dtype),
        ),
        in_specs=[pl.BlockSpec(memory_space=VMEM)] * 2,
        out_specs=(pl.BlockSpec(memory_space=VMEM), pl.BlockSpec(memory_space=VMEM)),
        scratch_shapes=[pltpu.SemaphoreType.DMA((slots,)), pltpu.SemaphoreType.DMA((slots,))],
        compiler_params=pltpu.CompilerParams(
            collective_id=5, has_side_effects=True, vmem_limit_bytes=40 << 20
        ),
        name="spread_rows",
    )(rows, share)


def collect_rows(partial):
    blocks, tall, wide = partial.shape
    count = blocks.bit_length() - 1
    half = wide // 2
    groups = 4
    w = half // groups
    stages = bits_of("seq") + bits_of("tp")
    slots = groups * (2 * count + 1)
    keys, scratch = [], []

    def reserve(key, *shape):
        keys.append(key)
        scratch.append(VMEM((*shape, tall, w), jnp.bfloat16))

    for g in range(groups):
        wide_at = 1 if g < groups // 2 else count
        for j in range(count):
            copies = 2 if j < wide_at else 1
            for h in range(copies):
                reserve(("got", g, j, h), blocks >> (j + 1))
            reserve(("sum", g, j), copies, blocks >> (j + 1))
        reserve(("got", g, "tp"), blocks >> wide_at)
        reserve(("sum", g, "tp"), 1, blocks >> wide_at)

    def kernel(part_ref, out_ref, *rest):
        buffers = dict(zip(keys, rest[:-2]))
        send_sem, recv_sem = rest[-2:]
        greet(stages)
        me, tp = lax.axis_index("seq"), lax.axis_index("tp")
        used = iter(range(slots))

        def send(source, target, stage):
            slot = next(used)
            return swap(source, target, send_sem.at[slot], recv_sem.at[slot], stage)

        def add(size, mine, base, got, out):
            def body(i, _):
                total = mine[base + i].astype(jnp.float32) + got[i].astype(jnp.float32)
                out[i] = total.astype(jnp.bfloat16)
                return 0

            lax.fori_loop(0, size, body, 0)

        def chain(g):
            wide_at = 1 if g < groups // 2 else count
            state = {
                "views": [part_ref.at[:, :, pl.ds(h * half + g * w, w)] for h in range(2)]
            }

            def seq_step(j, copies):
                size = blocks >> (j + 1)
                mine = bit(me, j)
                copying = []

                def start():
                    for h in range(copies):
                        away = state["views"][h].at[pl.ds((1 - mine) * size, size)]
                        copying.append(send(away, buffers["got", g, j, h], ("seq", j)))

                def end():
                    out = buffers["sum", g, j]
                    for h in range(copies):
                        copying[h].wait()
                        add(size, state["views"][h], mine * size, buffers["got", g, j, h], out.at[h])
                    state["both"] = out
                    state["views"] = [out.at[h] for h in range(copies)]

                price = {"z": 1.0 * size, "x": size, "c": 0.3 * size}[carrier(("seq", j))]
                return (("seq", j), max(2.0, price) * copies, start, end)

            def tp_step():
                size = blocks >> wide_at
                copying = []

                def start():
                    away = state["both"].at[1 - tp]
                    copying.append(send(away, buffers["got", g, "tp"], ("tp", 0)))

                def end():
                    copying[0].wait()
                    out = buffers["sum", g, "tp"]
                    add(size, state["both"].at[tp], 0, buffers["got", g, "tp"], out.at[0])
                    state["views"] = [out.at[0]]

                return (("tp", 0), size, start, end)

            steps = [seq_step(j, 2 if j < wide_at else 1) for j in range(count)]
            steps.insert(wide_at, tp_step())
            return steps, state

        made = [chain(g) for g in range(groups)]
        advance([steps for steps, _ in made])
        for g, (_, state) in enumerate(made):
            out_ref[:, g * w : (g + 1) * w] = state["views"][0][0].astype(jnp.float32)

    return pl.pallas_call(
        kernel,
        out_shape=jax.ShapeDtypeStruct((tall, half), jnp.float32),
        in_specs=[pl.BlockSpec(memory_space=VMEM)],
        out_specs=pl.BlockSpec(memory_space=VMEM),
        scratch_shapes=scratch
        + [pltpu.SemaphoreType.DMA((slots,)), pltpu.SemaphoreType.DMA((slots,))],
        compiler_params=pltpu.CompilerParams(
            collective_id=6, has_side_effects=True, vmem_limit_bytes=56 << 20
        ),
        name="collect_rows",
    )(partial)


def attention(query, prefix_keys, prefix_values, suffix, bias):
    tall, wide = query.shape
    heads = wide // HD
    cached = prefix_keys.shape[0]
    keys = bias.shape[1]
    many = len(suffix)
    scale = HD ** (-0.5)

    def kernel(query_ref, cached_k, cached_v, bias_ref, *rest):
        suffix_k, suffix_v, out_ref = rest[:many], rest[many : 2 * many], rest[2 * many]
        head = query_ref[...]
        scores = [
            lax.dot_general(
                head, block[...], (((1,), (1,)), ((), ())), preferred_element_type=jnp.float32
            )
            for block in (cached_k, *suffix_k)
        ]
        scores = jnp.concatenate(scores, 1) * scale + bias_ref[...]
        weights = jnp.exp(scores - jnp.max(scores, -1, keepdims=True))
        total = jnp.sum(weights, -1, keepdims=True)
        weights = weights.astype(jnp.bfloat16)
        summed = jnp.dot(weights[:, :cached], cached_v[...], preferred_element_type=jnp.float32)
        for n, block in enumerate(suffix_v):
            start = cached + n * tall
            summed += jnp.dot(
                weights[:, start : start + tall], block[...], preferred_element_type=jnp.float32
            )
        out_ref[...] = (summed / total).astype(jnp.bfloat16)

    def column(rows, offset):
        return pl.BlockSpec((rows, HD), lambda h: (0, h + offset))

    return pl.pallas_call(
        kernel,
        out_shape=jax.ShapeDtypeStruct((tall, wide), jnp.bfloat16),
        grid=(heads,),
        in_specs=[column(tall, 0), column(cached, 0), column(cached, 0)]
        + [pl.BlockSpec((tall, keys), lambda h: (0, 0))]
        + [column(tall, 0)] * many
        + [column(tall, heads)] * many,
        out_specs=column(tall, 0),
        cost_estimate=pl.CostEstimate(
            flops=4 * tall * keys * wide, bytes_accessed=4 * keys * wide, transcendentals=0
        ),
        name="attention",
    )(query, prefix_keys, prefix_values, bias, *suffix, *suffix)


def on_device(
    tokens,
    attn_gain,
    w_query,
    w_key,
    w_value,
    w_out,
    prefix_keys,
    prefix_values,
    shard_group,
    request_group,
    lengths,
    moe_gain,
    w_router,
    w_gate,
    w_up,
    w_down,
    routes,
    final_gain,
    w_head,
):
    f32 = jnp.float32
    bf16 = jnp.bfloat16
    seq_index = lax.axis_index("seq")
    tp_index = lax.axis_index("tp")
    seq_count = lax.axis_size("seq")
    tp_count = lax.axis_size("tp")
    tok_dev = tokens.shape[0]
    width_part = tokens.shape[1]
    shard_rows = prefix_keys.shape[0]
    prefix_length = shard_rows * seq_count // 2
    full_x, cached_k, cached_v = gather_front(tokens, prefix_keys, prefix_values)
    width = full_x.shape[1]
    normed = normalize(full_x.astype(f32), attn_gain).astype(bf16)
    heads = w_query.shape[1] // HD
    ends = jnp.cumsum(lengths)
    starts = ends - lengths
    local_index = seq_index * tok_dev + jnp.arange(tok_dev)
    own_request = request_of(local_index, ends)
    own_start = lookup(own_request, starts)
    own_group = lookup(own_request, request_group)
    position = (prefix_length + local_index - own_start).astype(f32)
    query = rotate(
        jnp.dot(normed, w_query, preferred_element_type=f32).reshape(tok_dev, heads, HD), position
    ).astype(bf16)
    key_rows = rotate(
        jnp.dot(normed, w_key, preferred_element_type=f32).reshape(tok_dev, heads, HD), position
    ).astype(bf16)
    key_rows = key_rows.reshape(tok_dev, heads * HD)
    value_rows = jnp.dot(normed, w_value, preferred_element_type=f32).astype(bf16)
    pieces = (
        cached_k.reshape(-1, heads * HD),
        cached_v.reshape(-1, heads * HD),
    )
    count = pieces[0].shape[0]
    shard_ids = jnp.arange(count) // shard_rows
    bits = seq_count.bit_length() - 1
    key_group = lookup(shard_ids, shard_group.reshape((2,) * bits).transpose().reshape(-1))
    fold_allowed = own_group[:, None] == key_group[None, :]
    own_allowed = (own_request[:, None] == own_request[None, :]) & (
        local_index[None, :] <= local_index[:, None]
    )
    both_rows = jnp.concatenate([key_rows, value_rows], 1)
    suffix = [both_rows] + [from_behind(both_rows, "seq", step) for step in range(1, SPAN + 1)]
    permitted = [fold_allowed, own_allowed]
    for step in range(1, SPAN + 1):
        key_index = (seq_index - step) * tok_dev + jnp.arange(tok_dev)
        key_request = request_of(key_index, ends)
        permitted.append(
            (key_index >= 0)[None, :] & (own_request[:, None] == key_request[None, :])
        )
    bias = jnp.where(jnp.concatenate(permitted, 1), 0.0, NEGATIVE)
    attended = attention(query.reshape(tok_dev, heads * HD), *pieces, suffix, bias)
    mixed = jnp.dot(attended, w_out, preferred_element_type=f32).astype(bf16)
    resid_full = (full_x.astype(f32) + sum_over_tp(mixed)).astype(bf16)
    moe_in = normalize(resid_full.astype(f32), moe_gain).astype(bf16)
    resid = lax.dynamic_slice_in_dim(resid_full, tp_index * width_part, width_part, 1)
    experts = w_router.shape[1]
    topk = routes.shape[1]
    probs = jax.nn.softmax(jnp.dot(moe_in, w_router, preferred_element_type=f32), -1)
    if 2 * topk >= experts and tp_count == 2:
        named = routes[:, :, None] == jnp.arange(experts)[None, None, :]
        share = jnp.sum(jnp.where(named, probs[:, None, :], 0.0), 1)
        blocks, shares = spread_rows(moe_in, share.T)
        own_share = lax.dynamic_slice_in_dim(shares, seq_index, 1, 1).reshape(-1, 1)
        rows = blocks.reshape(-1, width)
        gate = jnp.dot(rows, w_gate[0], preferred_element_type=f32)
        up = jnp.dot(rows, w_up[0], preferred_element_type=f32)
        act = (jax.nn.silu(gate) * up).astype(bf16)
        partial_out = (jnp.dot(act, w_down[0], preferred_element_type=f32) * own_share).astype(bf16)
        moe_part = collect_rows(partial_out.reshape(seq_count, tok_dev, width))
    else:
        flat = routes.reshape(-1)
        hits = (flat[:, None] == jnp.arange(experts)[None, :]).astype(jnp.int32)
        rank = jnp.sum((jnp.cumsum(hits, 0) - hits) * hits, 1)
        capacity = min(tok_dev, tp_count * max(1, 3 * tok_dev * topk // (2 * experts * tp_count)))
        target = flat * capacity + rank
        route_weight = jnp.sum(hits.reshape(tok_dev, topk, experts).astype(f32) * probs[:, None, :], -1)
        repeated = jnp.repeat(moe_in, topk, axis=0)
        outgoing = (
            jnp.zeros((experts * capacity, width), bf16)
            .at[target]
            .set(repeated)
            .reshape(experts, capacity, width)
        )
        arrived = lax.all_to_all(outgoing, "seq", split_axis=0, concat_axis=0, tiled=True)
        sources = arrived.shape[0]
        count = arrived.shape[1]
        rows = arrived.reshape(sources * count, width)
        gate = jnp.dot(rows, w_gate[0], preferred_element_type=f32)
        up = jnp.dot(rows, w_up[0], preferred_element_type=f32)
        act = (jax.nn.silu(gate) * up).astype(bf16)
        partial_out = jnp.dot(act, w_down[0], preferred_element_type=f32).reshape(sources, count, width)
        summed = lax.psum_scatter(partial_out, "tp", scatter_dimension=2, tiled=True).astype(bf16)
        returned = lax.all_to_all(summed, "seq", split_axis=0, concat_axis=0, tiled=True)
        picked = returned.reshape(experts * capacity, width_part)[target].reshape(
            tok_dev, topk, width_part
        )
        moe_part = jnp.sum(picked.astype(f32) * route_weight[:, :, None], 1)
    hidden = (resid.astype(f32) + moe_part).astype(bf16)
    last_hit = ((ends - 1)[:, None] == local_index[None, :]).astype(bf16)
    chosen = jnp.dot(last_hit, hidden, preferred_element_type=f32)
    final = last_rows(chosen, final_gain, width)
    log_probs = log_softmax(jnp.dot(final, w_head, preferred_element_type=f32))
    return (hidden, log_probs)


def solution(mesh):
    in_specs = (
        P("seq", "tp"),
        P(),
        P(None, "tp"),
        P(None, "tp"),
        P(None, "tp"),
        P("tp", None),
        P("seq", "tp"),
        P("seq", "tp"),
        P(),
        P(),
        P(),
        P(),
        P(),
        P("seq", None, "tp"),
        P("seq", None, "tp"),
        P("seq", "tp", None),
        P("seq", None),
        P("tp"),
        P("tp", "seq"),
    )
    out_specs = (P("seq", "tp"), P(None, "seq"))
    return jax.shard_map(
        on_device, mesh=mesh, in_specs=in_specs, out_specs=out_specs, check_vma=False
    )
```

```python
import heapq
import jax
import jax.numpy as jnp
from jax import lax
from jax.experimental import pallas as pl
from jax.experimental.pallas import tpu as pltpu
from jax.sharding import PartitionSpec as P

HD = 128
SPAN = 4
VMEM = pltpu.VMEM


EPS = 1e-05
NEGATIVE = -1e30


def from_behind(value, axis, steps):
    count = lax.axis_size(axis)
    leading, last = (max(0, -steps), min(count, count - steps))
    return lax.ppermute(value, axis, [(source, source + steps) for source in range(leading, last)])


def normalize(rows, gain):
    inv = lax.rsqrt(jnp.mean(rows * rows, -1, keepdims=True) + EPS)
    return rows * inv * gain.astype(jnp.float32)


def rotate(vectors, position):
    half = vectors.shape[-1] // 2
    freq = 10000.0 ** (-jnp.arange(half).astype(jnp.float32) / half)
    angle = position[:, None] * freq[None, :]
    cosine = jnp.cos(angle)[:, None, :]
    sine = jnp.sin(angle)[:, None, :]
    first = vectors[..., :half]
    second = vectors[..., half:]
    return jnp.concatenate([first * cosine - second * sine, second * cosine + first * sine], -1)


def request_of(index, ends):
    return jnp.sum((index[:, None] >= ends[None, :]).astype(jnp.int32), 1)


def lookup(selector, table):
    hit = selector[:, None] == jnp.arange(table.shape[0])[None, :]
    return jnp.sum(jnp.where(hit, table[None, :], 0), 1)


def partner(axis, bit):
    index = lax.axis_index(axis)
    span = 1 << bit
    other = index + span - 2 * span * ((index // span) % 2)
    return {axis: other}


def greet(stages):
    barrier = pltpu.get_barrier_semaphore()
    for axis, bit in stages:
        pl.semaphore_signal(barrier, inc=1, device_id=partner(axis, bit))
    pl.semaphore_wait(barrier, len(stages))


def swap(source, target, send_sem, recv_sem, stage):
    copy = pltpu.make_async_remote_copy(
        src_ref=source, dst_ref=target, send_sem=send_sem, recv_sem=recv_sem,
        device_id=partner(*stage),
    )
    copy.start()
    return copy


def bits_of(axis):
    return [(axis, bit) for bit in range(lax.axis_size(axis).bit_length() - 1)]


def head_tail(chosen, gain, w_head, width):
    seq_stages, tp_stages = bits_of("seq"), bits_of("tp")
    stages = seq_stages + tp_stages
    rows, part = chosen.shape
    vocab = w_head.shape[1]
    ns, nt = len(seq_stages), len(tp_stages)

    def kernel(chosen_ref, gain_ref, head_hbm, out_ref, head, rows_held, rows_got, sq_held, sq_got,
               lg_held, lg_got, st_held, st_got, head_sem, send_sem, recv_sem):
        loading = pltpu.make_async_copy(head_hbm, head, head_sem)
        loading.start()
        greet(stages)
        used = iter(range(2 * ns + 2 * nt))

        def exchange(held, got, k, stage):
            n = next(used)
            swap(held.at[k], got.at[k], send_sem.at[n], recv_sem.at[n], stage).wait()

        rows_held[0] = chosen_ref[...]
        for k, stage in enumerate(seq_stages):
            exchange(rows_held, rows_got, k, stage)
            rows_held[k + 1] = rows_held[k] + rows_got[k]
        last = rows_held[ns]
        sq_held[0] = jnp.broadcast_to(jnp.sum(last * last, -1, keepdims=True), (rows, 128))
        for k, stage in enumerate(tp_stages):
            exchange(sq_held, sq_got, k, stage)
            sq_held[k + 1] = sq_held[k] + sq_got[k]
        square = sq_held[nt][:, :1]
        final = last * lax.rsqrt(square / width + EPS) * gain_ref[...].astype(jnp.float32)
        final = final.astype(jnp.bfloat16)
        loading.wait()
        lg_held[0] = jnp.dot(final, head[...], preferred_element_type=jnp.float32)
        for k, stage in enumerate(tp_stages):
            exchange(lg_held, lg_got, k, stage)
            lg_held[k + 1] = lg_held[k] + lg_got[k]
        logits = lg_held[nt]
        peak = jnp.max(logits, -1, keepdims=True)
        mass = jnp.sum(jnp.exp(logits - peak), -1, keepdims=True)
        st_held[0, :, :128] = jnp.broadcast_to(peak, (rows, 128))
        st_held[0, :, 128:] = jnp.broadcast_to(mass, (rows, 128))
        for k, stage in enumerate(seq_stages):
            exchange(st_held, st_got, k, stage)
            mine, theirs = st_held[k, :, :128], st_got[k, :, :128]
            top = jnp.maximum(mine, theirs)
            st_held[k + 1, :, :128] = top
            st_held[k + 1, :, 128:] = st_held[k, :, 128:] * jnp.exp(mine - top) + st_got[
                k, :, 128:
            ] * jnp.exp(theirs - top)
        out_ref[...] = logits - st_held[ns, :, :1] - jnp.log(st_held[ns, :, 128:129])

    f32 = jnp.float32
    slots = 2 * ns + 2 * nt
    return pl.pallas_call(
        kernel,
        out_shape=jax.ShapeDtypeStruct((rows, vocab), f32),
        in_specs=[pl.BlockSpec(memory_space=VMEM)] * 2 + [pl.BlockSpec(memory_space=pl.ANY)],
        out_specs=pl.BlockSpec(memory_space=VMEM),
        scratch_shapes=[
            VMEM(w_head.shape, w_head.dtype),
            VMEM((ns + 1, rows, part), f32),
            VMEM((ns, rows, part), f32),
            VMEM((nt + 1, rows, 128), f32),
            VMEM((nt, rows, 128), f32),
            VMEM((nt + 1, rows, vocab), f32),
            VMEM((nt, rows, vocab), f32),
            VMEM((ns + 1, rows, 256), f32),
            VMEM((ns, rows, 256), f32),
            pltpu.SemaphoreType.DMA,
            pltpu.SemaphoreType.DMA((slots,)),
            pltpu.SemaphoreType.DMA((slots,)),
        ],
        compiler_params=pltpu.CompilerParams(
            collective_id=1, has_side_effects=True, vmem_limit_bytes=40 << 20
        ),
        name="head_tail",
    )(chosen, gain.reshape(1, part), w_head)


def gather_front(block, *cached):
    stages = bits_of("tp")
    rows, part = block.shape
    tp_count = lax.axis_size("tp")
    count = lax.axis_size("seq").bit_length() - 1
    many = len(cached)
    slots = many * count + len(stages)

    def kernel(block_ref, *rest):
        cached_refs, out_ref, outs = rest[:many], rest[many], rest[many + 1 : 2 * many + 1]
        send_sem, recv_sem = rest[-2:]
        me = lax.axis_index("tp")
        place = reversed_index(count)
        out_ref[:, pl.ds(pl.multiple_of(me * part, part), part)] = block_ref[...]
        for source, target in zip(cached_refs, outs):
            target[place] = source[...]
        greet(stages + bits_of("seq"))
        used = iter(range(slots))

        def send(piece, stage):
            slot = next(used)
            return swap(piece, piece, send_sem.at[slot], recv_sem.at[slot], stage)

        def tp_step(k, stage):
            wide = part << k
            start_at = pl.multiple_of((me // (1 << k)) * wide, wide)
            flying = []
            return (
                stage,
                4.0,
                lambda: flying.append(send(out_ref.at[:, pl.ds(start_at, wide)], stage)),
                lambda: flying[0].wait(),
            )

        chains = [[tp_step(k, stage) for k, stage in enumerate(stages)]]
        for target in outs:
            def view(j, _, target=target):
                return target.at[pl.ds((place // (1 << j)) * (1 << j), 1 << j)]

            chains.append(doubling(count, [], view, send))
        advance(chains)

    shapes = [jax.ShapeDtypeStruct((rows, part * tp_count), block.dtype)]
    for one in cached:
        shapes.append(jax.ShapeDtypeStruct((1 << count, *one.shape), one.dtype))
    return pl.pallas_call(
        kernel,
        out_shape=tuple(shapes),
        in_specs=[pl.BlockSpec(memory_space=VMEM)] * (1 + many),
        out_specs=tuple(pl.BlockSpec(memory_space=VMEM) for _ in shapes),
        scratch_shapes=[pltpu.SemaphoreType.DMA((slots,))] * 2,
        compiler_params=pltpu.CompilerParams(collective_id=3, has_side_effects=True),
        name="gather_front",
    )(block, *cached)


def sum_over_tp(block):
    stages = bits_of("tp")
    rows, part = block.shape

    def kernel(block_ref, out_ref, held, got, send_sem, recv_sem):
        greet(stages)
        for k, stage in enumerate(stages):
            source = block_ref if k == 0 else held.at[k]
            swap(source, got.at[k], send_sem.at[k], recv_sem.at[k], stage).wait()
            total = source[...].astype(jnp.float32) + got[k].astype(jnp.float32)
            if k + 1 < len(stages):
                held[k + 1] = total.astype(jnp.bfloat16)
            else:
                out_ref[...] = total

    count = len(stages)
    return pl.pallas_call(
        kernel,
        out_shape=jax.ShapeDtypeStruct((rows, part), jnp.float32),
        in_specs=[pl.BlockSpec(memory_space=VMEM)],
        out_specs=pl.BlockSpec(memory_space=VMEM),
        scratch_shapes=[
            VMEM((count, rows, part), jnp.bfloat16),
            VMEM((count, rows, part), jnp.bfloat16),
            pltpu.SemaphoreType.DMA((count,)),
            pltpu.SemaphoreType.DMA((count,)),
        ],
        compiler_params=pltpu.CompilerParams(collective_id=4, has_side_effects=True),
        name="sum_over_tp",
    )(block)


def bit(index, place):
    return (index // (1 << place)) % 2


def reversed_index(count):
    me = lax.axis_index("seq")
    return sum(bit(me, k) * (1 << (count - 1 - k)) for k in range(count))


def carrier(stage):
    axis, place = stage
    return "y" if axis == "tp" else "cxz"[min(place, 2)]


def advance(chains):
    left = [sum(step[1] for step in chain) for chain in chains]
    place, busy, events = [0] * len(chains), set(), []
    waiting, now = set(range(len(chains))), 0.0
    while waiting or events:
        for c in sorted(waiting, key=lambda c: (-left[c], c)):
            stage, cost, start, _ = chains[c][place[c]]
            if carrier(stage) not in busy:
                start()
                if carrier(stage) != "c":
                    busy.add(carrier(stage))
                waiting.remove(c)
                heapq.heappush(events, (now + cost, c))
        now, c = heapq.heappop(events)
        stage, cost, _, end = chains[c][place[c]]
        end()
        busy.discard(carrier(stage))
        left[c] -= cost
        place[c] += 1
        if place[c] < len(chains[c]):
            waiting.add(c)


def doubling(count, axis_hops, view, send):
    steps = []
    plan = [(("seq", count - 1 - j), j, None) for j in range(count)]
    plan[count - 1 : count - 1] = axis_hops
    for stage, j, columns in plan:
        flying = []

        def start(stage=stage, j=j, columns=columns, flying=flying):
            flying.append(send(view(j, columns), stage))

        price = {"z": max(2.0, 1.0 * (1 << j)), "x": 1 << j, "y": 1 << j, "c": 0.1 * (1 << j)}[
            carrier(stage)
        ]
        steps.append((stage, price, start, lambda flying=flying: flying[0].wait()))
    return steps


def take_turns(chains):
    for turn in range(max(len(chain) for chain in chains)):
        for chain in chains:
            if turn < len(chain):
                chain[turn]()


def spread_rows(rows, share):
    count = lax.axis_size("seq").bit_length() - 1
    blocks = 1 << count
    tall, wide = rows.shape
    quarter = wide // 4
    experts = share.shape[0]
    stages = bits_of("seq") + bits_of("tp")
    slots = 4 * count + 1

    def kernel(rows_ref, share_ref, out_ref, share_out, send_sem, recv_sem):
        place = reversed_index(count)
        tp = lax.axis_index("tp")
        out_ref[place] = rows_ref[...]
        share_out[place] = share_ref[...]
        greet(stages)
        used = iter(range(slots))
        flying = {}

        def hop(name, stage, view):
            def act():
                if name in flying:
                    flying[name].wait()
                slot = next(used)
                piece = view()
                flying[name] = swap(piece, piece, send_sem.at[slot], recv_sem.at[slot], stage)

            return act

        def span_of(j):
            return pl.ds((place // (1 << j)) * (1 << j), 1 << j)

        def rows_view(j, start, size):
            return lambda: out_ref.at[span_of(j), :, pl.ds(start, size)]

        own = pl.multiple_of(tp * quarter, quarter)
        crossing = [
            hop("q", ("seq", count - 1 - j), rows_view(j, own, quarter)) for j in range(count - 1)
        ]
        crossing.append(hop("q", ("tp", 0), rows_view(count - 1, own, quarter)))
        crossing.append(hop("q", ("seq", 0), rows_view(count - 1, 0, 2 * quarter)))
        chains = [crossing]
        for part in (2, 3):
            chains.append([
                hop(part, ("seq", count - 1 - j), rows_view(j, part * quarter, quarter))
                for j in range(count)
            ])
        chains.append([
            hop("s", ("seq", count - 1 - j), lambda j=j: share_out.at[span_of(j)])
            for j in range(count)
        ])
        take_turns(chains)
        for copy in flying.values():
            copy.wait()

    return pl.pallas_call(
        kernel,
        out_shape=(
            jax.ShapeDtypeStruct((blocks, tall, wide), rows.dtype),
            jax.ShapeDtypeStruct((blocks, experts, tall), share.dtype),
        ),
        in_specs=[pl.BlockSpec(memory_space=VMEM)] * 2,
        out_specs=(pl.BlockSpec(memory_space=VMEM), pl.BlockSpec(memory_space=VMEM)),
        scratch_shapes=[pltpu.SemaphoreType.DMA((slots,)), pltpu.SemaphoreType.DMA((slots,))],
        compiler_params=pltpu.CompilerParams(
            collective_id=5, has_side_effects=True, vmem_limit_bytes=40 << 20
        ),
        name="spread_rows",
    )(rows, share)


def collect_rows(partial):
    blocks, tall, wide = partial.shape
    count = blocks.bit_length() - 1
    half = wide // 2
    groups = 4
    w = half // groups
    stages = bits_of("seq") + bits_of("tp")
    slots = groups * (2 * count + 1)
    keys, scratch = [], []

    def reserve(key, *shape):
        keys.append(key)
        scratch.append(VMEM((*shape, tall, w), jnp.bfloat16))

    for g in range(groups):
        wide_at = 1 if g < groups // 2 else count
        for j in range(count):
            copies = 2 if j < wide_at else 1
            for h in range(copies):
                reserve(("got", g, j, h), blocks >> (j + 1))
            reserve(("sum", g, j), copies, blocks >> (j + 1))
        reserve(("got", g, "tp"), blocks >> wide_at)
        reserve(("sum", g, "tp"), 1, blocks >> wide_at)

    def kernel(part_ref, out_ref, *rest):
        buffers = dict(zip(keys, rest[:-2]))
        send_sem, recv_sem = rest[-2:]
        greet(stages)
        me, tp = lax.axis_index("seq"), lax.axis_index("tp")
        used = iter(range(slots))

        def send(source, target, stage):
            slot = next(used)
            return swap(source, target, send_sem.at[slot], recv_sem.at[slot], stage)

        def add(size, mine, base, got, out):
            def body(i, _):
                total = mine[base + i].astype(jnp.float32) + got[i].astype(jnp.float32)
                out[i] = total.astype(jnp.bfloat16)
                return 0

            lax.fori_loop(0, size, body, 0)

        def chain(g):
            wide_at = 1 if g < groups // 2 else count
            state = {
                "views": [part_ref.at[:, :, pl.ds(h * half + g * w, w)] for h in range(2)]
            }

            def seq_step(j, copies):
                size = blocks >> (j + 1)
                mine = bit(me, j)
                copying = []

                def start():
                    for h in range(copies):
                        away = state["views"][h].at[pl.ds((1 - mine) * size, size)]
                        copying.append(send(away, buffers["got", g, j, h], ("seq", j)))

                def end():
                    out = buffers["sum", g, j]
                    for h in range(copies):
                        copying[h].wait()
                        add(size, state["views"][h], mine * size, buffers["got", g, j, h], out.at[h])
                    state["both"] = out
                    state["views"] = [out.at[h] for h in range(copies)]

                price = {"z": 1.0 * size, "x": size, "c": 0.1 * size}[carrier(("seq", j))]
                price = price if carrier(("seq", j)) != "z" else max(2.0, price)
                return (("seq", j), price * copies, start, end)

            def tp_step():
                size = blocks >> wide_at
                copying = []

                def start():
                    away = state["both"].at[1 - tp]
                    copying.append(send(away, buffers["got", g, "tp"], ("tp", 0)))

                def end():
                    copying[0].wait()
                    out = buffers["sum", g, "tp"]
                    add(size, state["both"].at[tp], 0, buffers["got", g, "tp"], out.at[0])
                    state["views"] = [out.at[0]]

                return (("tp", 0), size, start, end)

            steps = [seq_step(j, 2 if j < wide_at else 1) for j in range(count)]
            steps.insert(wide_at, tp_step())
            return steps, state

        made = [chain(g) for g in range(groups)]
        advance([steps for steps, _ in made])
        for g, (_, state) in enumerate(made):
            out_ref[:, g * w : (g + 1) * w] = state["views"][0][0].astype(jnp.float32)

    return pl.pallas_call(
        kernel,
        out_shape=jax.ShapeDtypeStruct((tall, half), jnp.float32),
        in_specs=[pl.BlockSpec(memory_space=VMEM)],
        out_specs=pl.BlockSpec(memory_space=VMEM),
        scratch_shapes=scratch
        + [pltpu.SemaphoreType.DMA((slots,)), pltpu.SemaphoreType.DMA((slots,))],
        compiler_params=pltpu.CompilerParams(
            collective_id=6, has_side_effects=True, vmem_limit_bytes=56 << 20
        ),
        name="collect_rows",
    )(partial)


def attention(query, prefix_keys, prefix_values, suffix, bias):
    tall, wide = query.shape
    heads = wide // HD
    cached = prefix_keys.shape[0]
    keys = bias.shape[1]
    many = len(suffix)
    scale = HD ** (-0.5)

    def kernel(query_ref, cached_k, cached_v, bias_ref, *rest):
        suffix_k, suffix_v, out_ref = rest[:many], rest[many : 2 * many], rest[2 * many]
        head = query_ref[...]
        scores = [
            lax.dot_general(
                head, block[...], (((1,), (1,)), ((), ())), preferred_element_type=jnp.float32
            )
            for block in (cached_k, *suffix_k)
        ]
        scores = jnp.concatenate(scores, 1) * scale + bias_ref[...]
        weights = jnp.exp(scores - jnp.max(scores, -1, keepdims=True))
        total = jnp.sum(weights, -1, keepdims=True)
        weights = weights.astype(jnp.bfloat16)
        summed = jnp.dot(weights[:, :cached], cached_v[...], preferred_element_type=jnp.float32)
        for n, block in enumerate(suffix_v):
            start = cached + n * tall
            summed += jnp.dot(
                weights[:, start : start + tall], block[...], preferred_element_type=jnp.float32
            )
        out_ref[...] = (summed / total).astype(jnp.bfloat16)

    def column(rows, offset):
        return pl.BlockSpec((rows, HD), lambda h: (0, h + offset))

    return pl.pallas_call(
        kernel,
        out_shape=jax.ShapeDtypeStruct((tall, wide), jnp.bfloat16),
        grid=(heads,),
        in_specs=[column(tall, 0), column(cached, 0), column(cached, 0)]
        + [pl.BlockSpec((tall, keys), lambda h: (0, 0))]
        + [column(tall, 0)] * many
        + [column(tall, heads)] * many,
        out_specs=column(tall, 0),
        cost_estimate=pl.CostEstimate(
            flops=4 * tall * keys * wide, bytes_accessed=4 * keys * wide, transcendentals=0
        ),
        name="attention",
    )(query, prefix_keys, prefix_values, bias, *suffix, *suffix)


def on_device(
    tokens,
    attn_gain,
    w_query,
    w_key,
    w_value,
    w_out,
    prefix_keys,
    prefix_values,
    shard_group,
    request_group,
    lengths,
    moe_gain,
    w_router,
    w_gate,
    w_up,
    w_down,
    routes,
    final_gain,
    w_head,
):
    f32 = jnp.float32
    bf16 = jnp.bfloat16
    seq_index = lax.axis_index("seq")
    tp_index = lax.axis_index("tp")
    seq_count = lax.axis_size("seq")
    tp_count = lax.axis_size("tp")
    tok_dev = tokens.shape[0]
    width_part = tokens.shape[1]
    shard_rows = prefix_keys.shape[0]
    prefix_length = shard_rows * seq_count // 2
    full_x, cached_k, cached_v = gather_front(tokens, prefix_keys, prefix_values)
    width = full_x.shape[1]
    normed = normalize(full_x.astype(f32), attn_gain).astype(bf16)
    heads = w_query.shape[1] // HD
    ends = jnp.cumsum(lengths)
    starts = ends - lengths
    local_index = seq_index * tok_dev + jnp.arange(tok_dev)
    own_request = request_of(local_index, ends)
    own_start = lookup(own_request, starts)
    own_group = lookup(own_request, request_group)
    position = (prefix_length + local_index - own_start).astype(f32)
    query = rotate(
        jnp.dot(normed, w_query, preferred_element_type=f32).reshape(tok_dev, heads, HD), position
    ).astype(bf16)
    key_rows = rotate(
        jnp.dot(normed, w_key, preferred_element_type=f32).reshape(tok_dev, heads, HD), position
    ).astype(bf16)
    key_rows = key_rows.reshape(tok_dev, heads * HD)
    value_rows = jnp.dot(normed, w_value, preferred_element_type=f32).astype(bf16)
    pieces = (
        cached_k.reshape(-1, heads * HD),
        cached_v.reshape(-1, heads * HD),
    )
    count = pieces[0].shape[0]
    shard_ids = jnp.arange(count) // shard_rows
    bits = seq_count.bit_length() - 1
    key_group = lookup(shard_ids, shard_group.reshape((2,) * bits).transpose().reshape(-1))
    fold_allowed = own_group[:, None] == key_group[None, :]
    own_allowed = (own_request[:, None] == own_request[None, :]) & (
        local_index[None, :] <= local_index[:, None]
    )
    both_rows = jnp.concatenate([key_rows, value_rows], 1)
    suffix = [both_rows] + [from_behind(both_rows, "seq", step) for step in range(1, SPAN + 1)]
    permitted = [fold_allowed, own_allowed]
    for step in range(1, SPAN + 1):
        key_index = (seq_index - step) * tok_dev + jnp.arange(tok_dev)
        key_request = request_of(key_index, ends)
        permitted.append(
            (key_index >= 0)[None, :] & (own_request[:, None] == key_request[None, :])
        )
    bias = jnp.where(jnp.concatenate(permitted, 1), 0.0, NEGATIVE)
    attended = attention(query.reshape(tok_dev, heads * HD), *pieces, suffix, bias)
    mixed = jnp.dot(attended, w_out, preferred_element_type=f32).astype(bf16)
    resid_full = (full_x.astype(f32) + sum_over_tp(mixed)).astype(bf16)
    moe_in = normalize(resid_full.astype(f32), moe_gain).astype(bf16)
    resid = lax.dynamic_slice_in_dim(resid_full, tp_index * width_part, width_part, 1)
    experts = w_router.shape[1]
    topk = routes.shape[1]
    probs = jax.nn.softmax(jnp.dot(moe_in, w_router, preferred_element_type=f32), -1)
    if 2 * topk >= experts and tp_count == 2:
        named = routes[:, :, None] == jnp.arange(experts)[None, None, :]
        share = jnp.sum(jnp.where(named, probs[:, None, :], 0.0), 1)
        blocks, shares = spread_rows(moe_in, share.T)
        own_share = lax.dynamic_slice_in_dim(shares, seq_index, 1, 1).reshape(-1, 1)
        rows = blocks.reshape(-1, width)
        gate = jnp.dot(rows, w_gate[0], preferred_element_type=f32)
        up = jnp.dot(rows, w_up[0], preferred_element_type=f32)
        act = (jax.nn.silu(gate) * up).astype(bf16)
        partial_out = (jnp.dot(act, w_down[0], preferred_element_type=f32) * own_share).astype(bf16)
        moe_part = collect_rows(partial_out.reshape(seq_count, tok_dev, width))
    else:
        flat = routes.reshape(-1)
        hits = (flat[:, None] == jnp.arange(experts)[None, :]).astype(jnp.int32)
        rank = jnp.sum((jnp.cumsum(hits, 0) - hits) * hits, 1)
        capacity = min(tok_dev, tp_count * max(1, 3 * tok_dev * topk // (2 * experts * tp_count)))
        target = flat * capacity + rank
        route_weight = jnp.sum(hits.reshape(tok_dev, topk, experts).astype(f32) * probs[:, None, :], -1)
        repeated = jnp.repeat(moe_in, topk, axis=0)
        outgoing = (
            jnp.zeros((experts * capacity, width), bf16)
            .at[target]
            .set(repeated)
            .reshape(experts, capacity, width)
        )
        arrived = lax.all_to_all(outgoing, "seq", split_axis=0, concat_axis=0, tiled=True)
        sources = arrived.shape[0]
        count = arrived.shape[1]
        rows = arrived.reshape(sources * count, width)
        gate = jnp.dot(rows, w_gate[0], preferred_element_type=f32)
        up = jnp.dot(rows, w_up[0], preferred_element_type=f32)
        act = (jax.nn.silu(gate) * up).astype(bf16)
        partial_out = jnp.dot(act, w_down[0], preferred_element_type=f32).reshape(sources, count, width)
        summed = lax.psum_scatter(partial_out, "tp", scatter_dimension=2, tiled=True).astype(bf16)
        returned = lax.all_to_all(summed, "seq", split_axis=0, concat_axis=0, tiled=True)
        picked = returned.reshape(experts * capacity, width_part)[target].reshape(
            tok_dev, topk, width_part
        )
        moe_part = jnp.sum(picked.astype(f32) * route_weight[:, :, None], 1)
    hidden = (resid.astype(f32) + moe_part).astype(bf16)
    last_hit = ((ends - 1)[:, None] == local_index[None, :]).astype(bf16)
    chosen = jnp.dot(last_hit, hidden, preferred_element_type=f32)
    log_probs = head_tail(chosen, final_gain, w_head, width)
    return (hidden, log_probs)


def solution(mesh):
    in_specs = (
        P("seq", "tp"),
        P(),
        P(None, "tp"),
        P(None, "tp"),
        P(None, "tp"),
        P("tp", None),
        P("seq", "tp"),
        P("seq", "tp"),
        P(),
        P(),
        P(),
        P(),
        P(),
        P("seq", None, "tp"),
        P("seq", None, "tp"),
        P("seq", "tp", None),
        P("seq", None),
        P("tp"),
        P("tp", "seq"),
    )
    out_specs = (P("seq", "tp"), P(None, "seq"))
    return jax.shard_map(
        on_device, mesh=mesh, in_specs=in_specs, out_specs=out_specs, check_vma=False
    )
```
